128 devices in a mesh: group: 16 (over z, x_hi, core), tensor: 8 (over x_lo, y).
Axes of the slice: x: 4 (x_hi: 2, x_lo: 2; x = x_hi * 2 + x_lo), y: 4, z: 4, core: 2. Of those that a mesh axis runs over, the one named last changes fastest.
Arguments:
- hidden_in: bfloat16 [4096, 4096], P(('group', 'tensor')), may hold values from -6 to 6
- queries: bfloat16 [4096, 4096], P('group', 'tensor'), may hold values from -72 to 72
- new_kv: bfloat16 [2, 4096, 1024], P(None, 'group', 'tensor'), may hold values from -6 to 6
- pool_codes: bfloat16 [2, 32768, 1024], P(None, 'group', 'tensor'), may hold values from -1 to 1
- pool_scales: float32 [2, 64, 8], P(None, 'group', 'tensor'), may hold values from 0.5 to 4
- block_table: int32 [16, 16], replicated, may hold values from 0 to 63, as said below
- prefix_blocks: int32 [16], replicated, may hold values from 8 to 16, as said below
- out_proj: bfloat16 [4096, 4096], P('tensor'), may hold values from -0.09375 to 0.09375
- norm_gain: float32 [4096], replicated, may hold values from 0.5 to 1.5
- expert_ids: int32 [4096, 2], P(('group', 'tensor')), may hold values from 0 to 7, all different within a row; in each aligned block of 32 rows (0 to 31, 32 to 63, ...) at most 12 rows name the same one
- expert_share: float32 [4096], P(('group', 'tensor')), may hold values from 0.1 to 0.9
- gate_proj: bfloat16 [8, 8192, 4096], P('tensor', 'group'), may hold values from -0.09375 to 0.09375
- up_proj: bfloat16 [8, 8192, 4096], P('tensor', 'group'), may hold values from -0.09375 to 0.09375
- down_proj: bfloat16 [8, 8192, 4096], P('tensor', 'group'), may hold values from -0.0625 to 0.0625
- new_slots: int32 [32], replicated, may hold values from 0 to 31, as said below
Outputs:
- layer_out: bfloat16 [4096, 4096], P(('group', 'tensor'))
- new_codes: bfloat16 [2, 4096, 1024], P(None, 'group', 'tensor')
- new_scales: bfloat16 [2, 32, 8], P(None, 'group', 'tensor')
The draws below stay inside these ranges and needn't reach their ends.
Inputs may be any that keep to these rules, and one draw needn't show every extreme that they name: `block_table`: an entry b is block b % 4 of owner group b // 4. The 16 entries of a group's row lie on 16 different owners; several groups may share the same blocks. A group's prefix is the first prefix_blocks[g] entries of its row. `expert_ids`: within the 32 rows of one device no expert is named by more than 12 rows. A permutation: the block of sequence q (q // 2 its group) goes to owner group new_slots[q] // 2; the 2 sequences of one group go to different owners.
All inputs are finite; a program needn't handle non-finite values. Where the reference program divides by a largest or mean magnitude, that divisor is 1e-20 or more.
Results may differ from the reference program's by a relative error of at most 0.0095.
Values may be sent and summed in bfloat16 or wider, within the bound.
No kernel may reach another device: no remote copies, remote signals or barrier semaphores. Data moves between devices by JAX's collectives and lax.ppermute only.
A program may use at most 128 MiB of HBM per device.

```python
import math
import jax
import jax.numpy as jnp
import numpy as np
from jax import lax

D = 4096
HEADS = 32
KV_HEADS = 8
HEAD_DIM = 128
EXPERTS = 8
TOP = 2
FF = 8192
SUFFIX = 128
SEQS = 2
PBLOCK = 512
POOL = 4
BLK_MAX = 16
TOK_DEV = 32
TOKENS = 4096
CAP = 12
N_GROUP = 16
N_TENSOR = 8


def attention_inputs(key):
    folded = jax.random.fold_in(key, 31)
    splits = jax.random.split(folded, 2)
    query_vals = jnp.clip(jax.random.normal(splits[0], (TOKENS, KV_HEADS, HEADS // KV_HEADS, HEAD_DIM), jnp.float32), -6.0, 6.0)
    pair_vals = jnp.clip(jax.random.normal(splits[1], (2, TOKENS, KV_HEADS, HEAD_DIM), jnp.float32), -6.0, 6.0)
    return (query_vals.reshape(TOKENS, HEADS * HEAD_DIM), pair_vals.reshape(2, TOKENS, KV_HEADS * HEAD_DIM))


def draw_queries(key, part):
    return attention_inputs(key)[0].astype(jnp.bfloat16)


def draw_new_kv(key, part):
    return attention_inputs(key)[1].astype(jnp.bfloat16)


def prefix_layout(key):
    folded = jax.random.fold_in(key, 53)
    splits = jax.random.split(folded, 7)
    owner_keys = jax.random.split(splits[0], N_GROUP)
    base_order = jax.vmap(lambda item: jax.random.permutation(item, POOL))(owner_keys)
    offsets = jax.random.randint(splits[1], (POOL,), 0, N_GROUP)
    length = jax.random.randint(splits[2], (POOL,), BLK_MAX // 2, BLK_MAX + 1)
    longest = jax.random.randint(splits[3], (), 0, POOL)
    length = jnp.where(jnp.arange(POOL) == longest, BLK_MAX, length)
    picked_prefix = jax.random.randint(splits[4], (N_GROUP,), 0, POOL)
    forced = jax.random.randint(splits[5], (), 0, N_GROUP)
    picked_prefix = jnp.where(jnp.arange(N_GROUP) == forced, longest, picked_prefix)
    owner_ids = jnp.arange(N_GROUP)
    goal = jax.random.randint(splits[6], (N_GROUP,), 0, POOL)
    goal = jnp.where(owner_ids == 0, 0, goal)
    goal = jnp.where(owner_ids == N_GROUP - 1, POOL - 1, goal)
    slot_order = (base_order - base_order[:, longest][:, None] + goal[:, None]) % POOL
    position = jnp.arange(BLK_MAX)
    owners = (offsets[picked_prefix][:, None] + position[None, :]) % N_GROUP
    block_rows = owners * POOL + slot_order[owners, picked_prefix[:, None]]
    return (block_rows.astype(jnp.int32), length[picked_prefix].astype(jnp.int32))


def draw_block_table(key, part):
    return prefix_layout(key)[0]


def draw_prefix_blocks(key, part):
    return prefix_layout(key)[1]


def draw_new_slots(key, part):
    folded = jax.random.fold_in(key, 71)
    splits = jax.random.split(folded, 2)
    offsets = jax.random.permutation(splits[0], N_GROUP)[:SEQS]
    group_keys = jax.random.split(splits[1], N_GROUP)
    orders = jax.vmap(lambda item: jax.random.permutation(item, SEQS))(group_keys)
    group_col = jnp.arange(N_GROUP)[:, None]
    owners = (group_col + offsets[None, :]) % N_GROUP
    global_slot = owners * SEQS + jnp.arange(SEQS)[None, :]
    result = jnp.zeros((N_GROUP, SEQS), jnp.int32).at[group_col, orders].set(global_slot)
    return result.reshape(-1).astype(jnp.int32)


def shard_levels(stream_key, dims, cuts, least, high):
    factor_of, own = 1.0, jax.random.fold_in(stream_key, 6)
    for axis_at, parts in cuts:
        heights = jnp.exp(jax.random.uniform(jax.random.fold_in(own, axis_at), (parts,), jnp.float32, least / len(cuts), high / len(cuts)))
        factor_of = factor_of * jnp.repeat(heights, dims[axis_at] // parts).reshape([-1 if axis == axis_at else 1 for axis in range(len(dims))])
    return factor_of


def routed_block(own_key, own, number, rows, amount, top, reach, slope):
    sequence = jax.random.permutation(own_key, amount)
    heavy_load, ordinary = shares(amount, rows * top, reach, slope, True), shares(amount, rows * top, reach, slope, False)
    places = jnp.arange(amount)

    def named(tallies, rotation):
        used = int((tallies > 0).sum())
        fixed = max(1, used // 4)
        moved = fixed + (places - fixed + rotation * (used - fixed)) % max(1, amount - fixed)
        return jnp.zeros((amount,), jnp.int32).at[sequence[jnp.where(places < fixed, places, moved)]].set(jnp.asarray(tallies, jnp.int32))

    tallies = jnp.where(number % 4 == 0, named(heavy_load, number // 4), named(ordinary, number - number // 4 - 1))
    mixed = jax.random.permutation(jax.random.fold_in(own, 3), amount)
    donor, taker = mixed[0:amount // 2 * 2:2], mixed[1:amount // 2 * 2:2]
    margin = jnp.minimum(tallies[donor] - 1, reach - tallies[taker]) // 2
    margin = jnp.where((donor == sequence[0]) | (taker == sequence[0]) | (tallies[taker] == 0), 0, jnp.maximum(margin, 0))
    moved = jax.random.randint(jax.random.fold_in(own, 4), (amount // 2,), 0, 1 << 20) % (margin + 1)
    tallies = tallies.at[donor].add(-moved).at[taker].add(moved)
    labels = jnp.searchsorted(jnp.cumsum(tallies), jnp.arange(rows * top), side="right").astype(jnp.int32)
    table = labels.reshape(top, rows).T
    table = table[jax.random.permutation(jax.random.fold_in(own, 1), rows)]
    rotation = jax.random.randint(jax.random.fold_in(own, 2), (rows, 1), 0, top)
    return jnp.take_along_axis(table, (jnp.arange(top)[None, :] + rotation) % top, axis=1)


def shares(number_of, total, bound, slope, full):
    portions = [(1 << 20) // math.isqrt(standing ** slope) + 1 for standing in range(1, number_of + 1)]
    largest = bound if full else min(bound, max(-(-total // number_of), total * portions[0] // sum(portions)))
    least = 1 if total - largest >= number_of - 1 else 0
    given, surplus = [largest] + [least] * (number_of - 1), total - largest - least * (number_of - 1)
    while surplus > 0:
        candidates = [i for i in range(1, number_of) if given[i] < largest] or [i for i in range(1, number_of) if given[i] < bound]
        whole, left = sum([portions[i] for i in candidates]), surplus
        for i in candidates:
            more = min(bound - given[i], max(1, left * portions[i] // whole), surplus)
            given[i] = given[i] + more
            surplus = surplus - more
    return np.array(given)


def bell_draw(rng, dims, deviation, limit, cuts=(), kind=jnp.bfloat16):
    factor_of = shard_levels(rng, dims, cuts, -0.22, 0.18) if cuts else 1.0
    values = jax.random.normal(rng, dims, jnp.float32) * deviation * factor_of
    return jnp.minimum(jnp.maximum(values, -limit), limit).astype(kind)


def setup_inputs(seed: int = 0) -> dict:
    keys = jax.random.split(jax.random.key(seed), 16)
    hidden_in = bell_draw(keys[0], (TOKENS, D), 1.0, 6.0, ((0, 128),))
    queries = draw_queries(jax.random.fold_in(keys[15], 71), 0)
    new_kv = draw_new_kv(jax.random.fold_in(keys[15], 71), 0)
    pool_codes = jnp.clip(jax.random.uniform(keys[3], (2, N_GROUP * POOL * PBLOCK, KV_HEADS * HEAD_DIM), jnp.float32, -1.0, 1.0) * shard_levels(keys[3], (2, N_GROUP * POOL * PBLOCK, KV_HEADS * HEAD_DIM), ((1, 16), (2, 8)), -0.4, 0.0), -1.0, 1.0).astype(jnp.bfloat16)
    pool_scales = jnp.clip(jnp.exp(math.log(4.0) - 2.0794415 * jax.random.uniform(keys[4], (2, N_GROUP * POOL, KV_HEADS), jnp.float32) ** shard_levels(keys[4], (2, N_GROUP * POOL, KV_HEADS), ((1, 16), (2, 8)), -0.2, 0.2)), 0.5, 4.0)
    block_table = draw_block_table(jax.random.fold_in(keys[15], 71), 0)
    prefix_blocks = draw_prefix_blocks(jax.random.fold_in(keys[15], 71), 0)
    out_proj = bell_draw(keys[7], (HEADS * HEAD_DIM, D), (HEADS * HEAD_DIM) ** -0.5, 0.09375, ((0, 8),))
    norm_gain = jnp.clip(1.0 + 0.1 * jax.random.normal(keys[8], (D,), jnp.float32), 0.5, 1.5)
    expert_ids_keys = jax.random.split(jax.random.fold_in(keys[9], 1), TOKENS // TOK_DEV)
    expert_ids_turns = jax.random.permutation(jax.random.fold_in(keys[9], 3), TOKENS // TOK_DEV)
    expert_ids = jax.vmap(lambda own, number: routed_block(jax.random.fold_in(keys[9], 2), own, number, TOK_DEV, EXPERTS, TOP, CAP, 2))(expert_ids_keys, expert_ids_turns).reshape((TOKENS, TOP))
    expert_share = jnp.clip(0.1 + 0.79999997 * jax.random.uniform(keys[10], (TOKENS,), jnp.float32) ** shard_levels(keys[10], (TOKENS,), ((0, 128),), -0.2, 0.2), 0.1, 0.9)
    gate_proj = bell_draw(keys[11], (EXPERTS, FF, D), D ** -0.5, 0.09375, ((0, 8), (1, 16)))
    up_proj = bell_draw(keys[12], (EXPERTS, FF, D), D ** -0.5, 0.09375, ((0, 8), (1, 16)))
    down_proj = bell_draw(keys[13], (EXPERTS, FF, D), FF ** -0.5, 0.0625, ((0, 8), (1, 16)))
    new_slots = draw_new_slots(jax.random.fold_in(keys[15], 71), 0)
    return {"hidden_in": hidden_in, "queries": queries, "new_kv": new_kv, "pool_codes": pool_codes, "pool_scales": pool_scales, "block_table": block_table, "prefix_blocks": prefix_blocks, "out_proj": out_proj, "norm_gain": norm_gain, "expert_ids": expert_ids, "expert_share": expert_share, "gate_proj": gate_proj, "up_proj": up_proj, "down_proj": down_proj, "new_slots": new_slots}


def attend(query_rows, prefix_keys, prefix_vals, prefix_live, suffix_keys, suffix_vals, per_kv, suffix):
    factor = 1.0 / math.sqrt(query_rows.shape[1])
    prefix_scores = jnp.dot(query_rows, prefix_keys.T, preferred_element_type=jnp.float32) * factor
    prefix_scores = jnp.where(prefix_live[None, :], prefix_scores, -1e+30)
    suffix_scores = jnp.dot(query_rows, suffix_keys.T, preferred_element_type=jnp.float32) * factor
    token_pos = lax.broadcasted_iota(jnp.int32, suffix_scores.shape, 0) // per_kv
    key_pos = lax.broadcasted_iota(jnp.int32, suffix_scores.shape, 1)
    visible = jnp.logical_and(token_pos // suffix == key_pos // suffix, key_pos <= token_pos)
    suffix_scores = jnp.where(visible, suffix_scores, -1e+30)
    highest = jnp.maximum(lax.optimization_barrier(jnp.max(prefix_scores, axis=1)), lax.optimization_barrier(jnp.max(suffix_scores, axis=1)))[:, None]
    prefix_exp = jnp.exp(prefix_scores - highest)
    suffix_exp = jnp.exp(suffix_scores - highest)
    total = lax.optimization_barrier(jnp.sum(prefix_exp, axis=1, keepdims=True)) + lax.optimization_barrier(jnp.sum(suffix_exp, axis=1, keepdims=True))
    prefix_weight = (prefix_exp / total).astype(jnp.bfloat16)
    suffix_weight = (suffix_exp / total).astype(jnp.bfloat16)
    return jnp.dot(prefix_weight, prefix_vals, preferred_element_type=jnp.float32) + jnp.dot(suffix_weight, suffix_vals, preferred_element_type=jnp.float32)

def reference(hidden_in, queries, new_kv, pool_codes, pool_scales, block_table, prefix_blocks, out_proj, norm_gain, expert_ids, expert_share, gate_proj, up_proj, down_proj, new_slots):
    group_tok = SEQS * SUFFIX
    per_kv = HEADS // KV_HEADS
    decoded = (pool_codes.astype(jnp.float32).reshape(2, N_GROUP * POOL, PBLOCK, KV_HEADS, HEAD_DIM) * pool_scales[:, :, None, :, None]).astype(jnp.bfloat16)

    def one_group(group):
        rows_used = block_table[group]
        picked = jnp.take(decoded, rows_used, axis=1)
        picked = picked.reshape(2, BLK_MAX * PBLOCK, KV_HEADS, HEAD_DIM).transpose(2, 0, 1, 3)
        live = jnp.repeat(jnp.arange(BLK_MAX, dtype=jnp.int32) < prefix_blocks[group], PBLOCK)
        first = (group * group_tok).astype(jnp.int32)
        query_part = lax.dynamic_slice_in_dim(queries, first, group_tok, 0)
        query_part = query_part.reshape(group_tok, KV_HEADS, per_kv * HEAD_DIM).transpose(1, 0, 2).reshape(KV_HEADS, group_tok * per_kv, HEAD_DIM)
        pair_part = lax.dynamic_slice_in_dim(new_kv, first, group_tok, 1)
        pair_part = pair_part.reshape(2, group_tok, KV_HEADS, HEAD_DIM).transpose(2, 0, 1, 3)

        def one_head(items):
            query_rows, prefix_pair, suffix_pair = items
            return attend(query_rows, prefix_pair[0], prefix_pair[1], live, suffix_pair[0], suffix_pair[1], per_kv, SUFFIX)
        head_out = lax.map(one_head, (query_part, picked, pair_part))
        head_out = head_out.reshape(KV_HEADS, group_tok, per_kv * HEAD_DIM).transpose(1, 0, 2)
        return head_out.reshape(group_tok, HEADS * HEAD_DIM).astype(jnp.bfloat16)
    attn = lax.map(one_group, jnp.arange(N_GROUP, dtype=jnp.int32)).reshape(N_GROUP * group_tok, HEADS * HEAD_DIM)
    resid = hidden_in.astype(jnp.float32) + jnp.dot(attn, out_proj, preferred_element_type=jnp.float32)
    normed = (resid * lax.rsqrt(lax.optimization_barrier(jnp.mean(resid * resid, axis=1, keepdims=True)) + 1e-05) * norm_gain).astype(jnp.bfloat16)
    tok_dev = group_tok // N_TENSOR
    devices = N_GROUP * N_TENSOR
    cap = CAP
    pairs = expert_ids.reshape(devices, tok_dev * TOP)
    onehot = (pairs[:, :, None] == jnp.arange(EXPERTS, dtype=jnp.int32)[None, None, :]).astype(jnp.int32)
    rank = lax.optimization_barrier(jnp.sum(onehot * (jnp.cumsum(onehot, axis=1) - 1), axis=2))
    slot = (jnp.arange(devices, dtype=jnp.int32)[:, None] * cap + rank).reshape(-1)
    expert_flat = pairs.reshape(-1)
    token_flat = jnp.repeat(jnp.arange(TOKENS, dtype=jnp.int32), TOP)
    buffers = jnp.zeros((EXPERTS, devices * cap, D), jnp.bfloat16).at[expert_flat, slot].set(normed[token_flat])
    ff_dev = FF // N_GROUP

    def one_expert(items):
        expert_rows, gate_w, up_w, down_w = items
        gate_part = jnp.dot(expert_rows, gate_w.T, preferred_element_type=jnp.float32)
        up_part = jnp.dot(expert_rows, up_w.T, preferred_element_type=jnp.float32)
        expert_hidden = (jax.nn.silu(gate_part) * up_part).astype(jnp.bfloat16)

        def add_slice(index, total):
            offset = (jnp.asarray(index).astype(jnp.int32) * ff_dev).astype(jnp.int32)
            part = lax.dynamic_slice_in_dim(expert_hidden, offset, ff_dev, 1)
            weights = lax.dynamic_slice_in_dim(down_w, offset, ff_dev, 0)
            rounded = jnp.dot(part, weights, preferred_element_type=jnp.float32).astype(jnp.bfloat16)
            rounded = lax.optimization_barrier(rounded)
            return total + rounded.astype(jnp.float32)
        return lax.fori_loop(0, N_GROUP, add_slice, jnp.zeros((devices * cap, D), jnp.float32))
    expert_out = lax.map(one_expert, (buffers, gate_proj, up_proj, down_proj))
    chosen = expert_out[expert_flat, slot].reshape(TOKENS, TOP, D)
    share = expert_share[:, None]
    layer_out = (resid + share * chosen[:, 0] + (1.0 - share) * chosen[:, 1]).astype(jnp.bfloat16)
    fresh = new_kv.astype(jnp.float32).reshape(2, N_GROUP * SEQS, SUFFIX, KV_HEADS, HEAD_DIM)
    store_scale = (lax.optimization_barrier(jnp.max(jnp.abs(fresh), axis=(2, 4))) + 1e-06).astype(jnp.bfloat16)
    store_codes = (fresh / store_scale[:, :, None, :, None].astype(jnp.float32)).astype(jnp.bfloat16)
    new_codes = jnp.zeros_like(store_codes).at[:, new_slots].set(store_codes)
    new_codes = new_codes.reshape(2, N_GROUP * SEQS * SUFFIX, KV_HEADS * HEAD_DIM)
    new_scales = jnp.zeros_like(store_scale).at[:, new_slots].set(store_scale)
    return (layer_out, new_codes, new_scales)
```

```python
import functools
import math

import jax
import jax.numpy as jnp
from jax import lax
from jax.experimental import pallas as pl
from jax.experimental.pallas import tpu as pltpu
from jax.sharding import Mesh
from jax.sharding import PartitionSpec as P

EXPERTS = 8
TOP = 2
SUFFIX = 128
CAP = 12
GROUP = ("z", "xh", "c")
TENSOR = ("xl", "y")
SPLIT = 2304


def shift_z(x, by):
    n = lax.axis_size("z")
    return lax.ppermute(x, "z", [(i, (i + by) % n) for i in range(n)])


def swap(x, axis):
    return lax.ppermute(x, axis, [(0, 1), (1, 0)])


def plus(*terms):
    return sum(t.astype(jnp.float32) for t in terms)


def select_body(picked, scale_ref, codes_ref, out_ref):
    g = pl.program_id(0)
    pool = scale_ref.shape[0] // 2
    at = picked[g]
    for c in range(2):
        s = scale_ref[c * pool + at]
        out_ref[0, c] = (codes_ref[c, 0].astype(jnp.float32) * s).astype(jnp.bfloat16)


def select_blocks(picked, scales, codes):
    _, pool, rows, width = codes.shape
    groups = picked.shape[0]
    return pl.pallas_call(
        select_body,
        grid_spec=pltpu.PrefetchScalarGridSpec(
            num_scalar_prefetch=1,
            grid=(groups,),
            in_specs=[
                pl.BlockSpec(memory_space=pltpu.SMEM),
                pl.BlockSpec((2, 1, rows, width), lambda g, p: (0, p[g], 0, 0)),
            ],
            out_specs=pl.BlockSpec((1, 2, rows, width), lambda g, p: (g, 0, 0, 0)),
        ),
        out_shape=jax.ShapeDtypeStruct((groups, 2, rows, width), jnp.bfloat16),
        cost_estimate=pl.CostEstimate(flops=4 << 20, bytes_accessed=8 << 20, transcendentals=0),
        name="select",
    )(picked, scales, codes)


def attend_body(live, q_ref, new_ref, kv_ref, out_ref, q_sc, m_sc, acc_sc, v_sc):
    step = pl.program_id(0)
    toks, dim = q_ref.shape[0], new_ref.shape[2]
    heads = q_ref.shape[1] // dim
    factor = math.log2(math.e) / math.sqrt(dim)
    nt = (((1,), (1,)), ((), ()))

    @pl.when(step == 0)
    def _():
        v_sc[:, dim:] = jnp.ones((v_sc.shape[0], dim), jnp.bfloat16)
        v_sc[:toks, :dim] = new_ref[1]
        tok = lax.broadcasted_iota(jnp.int32, (toks, toks), 0)
        key = lax.broadcasted_iota(jnp.int32, (toks, toks), 1)
        seen = jnp.logical_and(tok // SUFFIX == key // SUFFIX, key <= tok)
        for h in range(heads):
            rows = slice(h * toks, (h + 1) * toks)
            q = q_ref[:, h * dim : (h + 1) * dim]
            q_sc[rows] = q
            s = lax.dot_general(q, new_ref[0], nt, preferred_element_type=jnp.float32)
            s = jnp.where(seen, s * factor, -1e30)
            m = jnp.max(s, axis=1, keepdims=True)
            p = jnp.exp2(s - m).astype(jnp.bfloat16)
            m_sc[rows] = jnp.broadcast_to(m, (toks, dim))
            acc_sc[rows] = jnp.dot(p, v_sc[:toks], preferred_element_type=jnp.float32)

    @pl.when(live[step] > 0)
    def _():
        v_sc[:, :dim] = kv_ref[0, 1]
        k = kv_ref[0, 0]
        for h in range(heads):
            rows = slice(h * toks, (h + 1) * toks)
            s = lax.dot_general(q_sc[rows], k, nt, preferred_element_type=jnp.float32) * factor
            old = m_sc[rows][:, :1]
            m = jnp.maximum(old, jnp.max(s, axis=1, keepdims=True))
            p = jnp.exp2(s - m).astype(jnp.bfloat16)
            m_sc[rows] = jnp.broadcast_to(m, (toks, dim))
            acc_sc[rows] = acc_sc[rows] * jnp.exp2(old - m) + jnp.dot(
                p, v_sc[...], preferred_element_type=jnp.float32
            )

    @pl.when(step == pl.num_programs(0) - 1)
    def _():
        for h in range(heads):
            rows = slice(h * toks, (h + 1) * toks)
            out_ref[:, h * dim : (h + 1) * dim] = (
                acc_sc[rows][:, :dim] / acc_sc[rows][:, dim:]
            ).astype(jnp.bfloat16)


def attention(live, queries, new_kv, got):
    owners, _, rows, dim = got.shape
    toks, width = queries.shape
    whole = lambda shape: pl.BlockSpec(shape, lambda i, p: (0,) * len(shape))
    total = width // dim * toks
    return pl.pallas_call(
        attend_body,
        grid_spec=pltpu.PrefetchScalarGridSpec(
            num_scalar_prefetch=1,
            grid=(owners,),
            in_specs=[
                whole(queries.shape),
                whole(new_kv.shape),
                pl.BlockSpec((1, 2, rows, dim), lambda i, p: (i, 0, 0, 0)),
            ],
            out_specs=whole(queries.shape),
            scratch_shapes=[
                pltpu.VMEM((total, dim), jnp.bfloat16),
                pltpu.VMEM((total, dim), jnp.float32),
                pltpu.VMEM((total, 2 * dim), jnp.float32),
                pltpu.VMEM((rows, 2 * dim), jnp.bfloat16),
            ],
        ),
        out_shape=jax.ShapeDtypeStruct(queries.shape, jnp.bfloat16),
        cost_estimate=pl.CostEstimate(
            flops=6 * total * rows * dim * owners,
            bytes_accessed=5 << 20,
            transcendentals=total * rows * owners,
        ),
        name="attend",
    )(live, queries, new_kv, got)


def store_body(pick, mine_ref, other_ref, codes_ref, scale_ref):
    k = pl.program_id(0)
    use_mine = pick[3 * k] == 0
    for c in range(2):
        x = jnp.where(use_mine, mine_ref[0, c], other_ref[0, c]).astype(jnp.float32)
        top = jnp.max(jnp.max(jnp.abs(x), axis=0, keepdims=True), axis=1, keepdims=True)
        scale = (top + 1e-06).astype(jnp.bfloat16).astype(jnp.float32)
        codes_ref[c] = (x / scale).astype(jnp.bfloat16)
        scale_ref[0, c : c + 1] = jnp.broadcast_to(scale, (1, scale_ref.shape[2]))


def store_blocks(pick, mine, other, seqs):
    _, _, rows, dim = mine.shape
    source = pl.BlockSpec((1, 2, SUFFIX, dim), lambda k, p: (p[3 * k + 1], 0, p[3 * k + 2], 0))
    return pl.pallas_call(
        store_body,
        grid_spec=pltpu.PrefetchScalarGridSpec(
            num_scalar_prefetch=1,
            grid=(seqs,),
            in_specs=[source, source],
            out_specs=[
                pl.BlockSpec((2, SUFFIX, dim), lambda k, p: (0, k, 0)),
                pl.BlockSpec((1, 2, dim), lambda k, p: (k, 0, 0)),
            ],
        ),
        out_shape=[
            jax.ShapeDtypeStruct((2, seqs * SUFFIX, dim), jnp.bfloat16),
            jax.ShapeDtypeStruct((seqs, 2, dim), jnp.float32),
        ],
        cost_estimate=pl.CostEstimate(flops=1 << 17, bytes_accessed=1 << 18, transcendentals=0),
        name="store",
    )(pick, mine, other)


def expert_body(moves_in, moves_out, chunk, *refs):
    n_in, n_out = len(moves_in), len(moves_out)
    ins, refs = refs[:n_in], refs[n_in:]
    own, other, refs = refs[:3], refs[3:6], refs[6:]
    outs, (x_sc, acc_sc, sem) = refs[:n_out], refs[n_out:]
    step, steps = pl.program_id(0), pl.num_programs(0)
    rows = x_sc.shape[0]
    nt = (((1,), (1,)), ((), ()))

    @pl.when(step == 0)
    def _():
        copies = []
        for i, (ref, (r, c)) in enumerate(zip(ins, moves_in)):
            dst = x_sc.at[pl.ds(r, ref.shape[0]), pl.ds(c, ref.shape[1])]
            copies.append(pltpu.make_async_copy(ref, dst, sem.at[i]))
        for copy in copies:
            copy.start()
        for copy in copies:
            copy.wait()

    def run(gate, up, down, first):
        for r in range(0, rows, chunk):
            x = x_sc[r : r + chunk]
            g = lax.dot_general(x, gate[0], nt, preferred_element_type=jnp.float32)
            u = lax.dot_general(x, up[0], nt, preferred_element_type=jnp.float32)
            h = (g / (1.0 + jnp.exp(-g)) * u).astype(jnp.bfloat16)
            y = jnp.dot(h, down[0], preferred_element_type=jnp.float32)
            if first is None:
                acc_sc[r : r + chunk] += y
            else:

                @pl.when(first)
                def _():
                    acc_sc[r : r + chunk] = y

                @pl.when(jnp.logical_not(first))
                def _():
                    acc_sc[r : r + chunk] += y

    @pl.when(step < steps // 2)
    def _():
        run(*own, step == 0)

    @pl.when(step >= steps // 2)
    def _():
        run(*other, None)

    @pl.when(step == steps - 1)
    def _():
        for ref, (r, c) in zip(outs, moves_out):
            ref[...] = acc_sc[r : r + ref.shape[0], c : c + ref.shape[1]].astype(jnp.bfloat16)


def experts(pieces, own, other, shapes_out, rows, tile=256, chunk=384):
    _, units, width = own[0].shape
    half = units // tile
    first = pl.BlockSpec((1, tile, width), lambda i: (0, jnp.minimum(i, half - 1), 0))
    second = pl.BlockSpec((1, tile, width), lambda i: (0, jnp.maximum(i - half, 0), 0))
    ins, moves_in = zip(*pieces)
    shapes, moves_out = zip(*shapes_out)
    return pl.pallas_call(
        functools.partial(expert_body, moves_in, moves_out, chunk),
        grid=(2 * half,),
        in_specs=[pl.BlockSpec(memory_space=pl.ANY)] * len(ins) + [first] * 3 + [second] * 3,
        out_specs=[pl.BlockSpec(s, lambda i: (0, 0)) for s in shapes],
        out_shape=[jax.ShapeDtypeStruct(s, jnp.bfloat16) for s in shapes],
        scratch_shapes=[
            pltpu.VMEM((rows, width), jnp.bfloat16),
            pltpu.VMEM((rows, width), jnp.float32),
            pltpu.SemaphoreType.DMA((len(ins),)),
        ],
        compiler_params=pltpu.CompilerParams(vmem_limit_bytes=64 << 20 if False else 66_000_000),
        cost_estimate=pl.CostEstimate(
            flops=12 * rows * units * width,
            bytes_accessed=12 * units * width + 4 * rows * width,
            transcendentals=2 * rows * units,
        ),
        name="experts",
    )(*ins, *own, *other)


def local(
    hidden_in,
    queries,
    new_kv,
    pool_codes,
    pool_scales,
    block_table,
    prefix_blocks,
    out_proj,
    norm_gain,
    expert_ids,
    expert_share,
    gate_proj,
    up_proj,
    down_proj,
    new_slots,
):
    groups = lax.axis_size(GROUP)
    tensors = lax.axis_size(TENSOR)
    n_z = lax.axis_size("z")
    my_group = lax.axis_index(GROUP)
    pool = pool_scales.shape[1]
    dim = pool_codes.shape[2]
    pblock = pool_codes.shape[1] // pool
    group_tok = queries.shape[0]
    seqs = group_tok // SUFFIX
    model_width = hidden_in.shape[1]

    owners = block_table // pool
    position = lax.broadcasted_iota(jnp.int32, block_table.shape, 1)
    mine = jnp.logical_and(owners == my_group, position < prefix_blocks[:, None])
    picked = jnp.sum(jnp.where(mine, block_table % pool, 0), axis=1)
    outgoing = select_blocks(
        picked, pool_scales.reshape(-1), pool_codes.reshape(2, pool, pblock, dim)
    )
    got = lax.all_to_all(outgoing, GROUP, split_axis=0, concat_axis=0, tiled=True)
    my_row = lax.dynamic_index_in_dim(block_table, my_group, 0, keepdims=False)
    my_length = lax.dynamic_index_in_dim(prefix_blocks, my_group, 0, keepdims=False)
    row_live = lax.broadcasted_iota(jnp.int32, my_row.shape, 0) < my_length
    owner_iota = lax.broadcasted_iota(jnp.int32, (groups, my_row.shape[0]), 0)
    live = jnp.any(
        jnp.logical_and((my_row // pool)[None, :] == owner_iota, row_live[None, :]), axis=1
    ).astype(jnp.int32)

    own = (gate_proj, up_proj, down_proj)
    own_late, fresh, got = lax.optimization_barrier((own, new_kv, got))
    other = tuple(swap(w, "c") for w in own_late)
    pair = jnp.stack([fresh, swap(fresh, "xh")])

    attn = attention(live, queries, new_kv, got)
    partial = jnp.dot(attn, out_proj, preferred_element_type=jnp.float32).astype(jnp.bfloat16)
    partial = partial.reshape(tensors, group_tok // tensors, model_width)
    ring = jnp.concatenate([pair] + [shift_z(pair, k) for k in range(1, n_z)])
    arrived = lax.all_to_all(partial, TENSOR, split_axis=0, concat_axis=0, tiled=True)
    resid = hidden_in.astype(jnp.float32) + arrived.astype(jnp.float32).sum(axis=0)
    normed = (
        resid * lax.rsqrt(jnp.mean(resid * resid, axis=1, keepdims=True) + 1e-05) * norm_gain
    ).astype(jnp.bfloat16)

    tok_dev = group_tok // tensors
    pair_ids = expert_ids.reshape(-1)
    onehot = (
        pair_ids[:, None] == lax.broadcasted_iota(jnp.int32, (pair_ids.shape[0], EXPERTS), 1)
    ).astype(jnp.int32)
    rank = jnp.sum(onehot * (jnp.cumsum(onehot, axis=0) - 1), axis=1)
    slot = (pair_ids * CAP + rank).reshape(tok_dev, TOP)
    slot_iota = lax.broadcasted_iota(jnp.int32, (EXPERTS * CAP,), 0)
    matches = slot[:, :, None] == slot_iota[None, None, :]
    route_rows = jnp.any(matches, axis=1).astype(jnp.bfloat16)
    pair_weight = jnp.stack([expert_share, 1.0 - expert_share], axis=1)
    combine = jnp.sum(jnp.where(matches, pair_weight[:, :, None], 0.0), axis=1)
    outbound = jnp.einsum(
        "ie,id->ed", route_rows, normed, preferred_element_type=jnp.float32
    ).astype(jnp.bfloat16)
    landed = lax.all_to_all(outbound, TENSOR, split_axis=0, concat_axis=0, tiled=True)

    n = landed.shape[0]
    a, b = landed[:, :SPLIT], landed[:, SPLIT:]
    wide = model_width - SPLIT
    half = wide // 2
    ax = swap(a, "xh")
    b_r, b_l = shift_z(b, 1), shift_z(b, -1)
    bx = swap(b, "xh")
    b_f1, b_f2 = shift_z(b_r[:, :half], 1), shift_z(b_l[:, half:], -1)
    a2 = jnp.concatenate([a, ax])
    a_r, a_l = shift_z(a2, 1), shift_z(a2, -1)
    bx_rl = swap(jnp.concatenate([b_r, b_l]), "xh")
    bx_f = swap(jnp.concatenate([b_f1, b_f2], axis=1), "xh")
    a_f1, a_f2 = shift_z(a_r[:n], 1), shift_z(a_l[n:], -1)

    pieces = [
        (a2, (0, 0)),
        (a_r, (2 * n, 0)),
        (a_l, (4 * n, 0)),
        (a_f1, (6 * n, 0)),
        (a_f2, (7 * n, 0)),
        (b, (0, SPLIT)),
        (bx, (n, SPLIT)),
        (b_r, (2 * n, SPLIT)),
        (bx_rl[:n], (3 * n, SPLIT)),
        (b_l, (4 * n, SPLIT)),
        (bx_rl[n:], (5 * n, SPLIT)),
        (b_f1, (6 * n, SPLIT)),
        (b_f2, (6 * n, SPLIT + half)),
        (bx_f, (7 * n, SPLIT)),
    ]
    shapes_out = [
        ((n, SPLIT), (6 * n, 0)),
        ((n, SPLIT), (7 * n, 0)),
        ((2 * n, SPLIT), (2 * n, 0)),
        ((2 * n, SPLIT), (4 * n, 0)),
        ((2 * n, SPLIT), (0, 0)),
        ((n, wide), (7 * n, SPLIT)),
        ((n, wide), (3 * n, SPLIT)),
        ((n, wide), (5 * n, SPLIT)),
        ((n, wide), (n, SPLIT)),
        ((n, wide), (6 * n, SPLIT)),
        ((n, wide), (2 * n, SPLIT)),
        ((n, wide), (4 * n, SPLIT)),
        ((n, wide), (0, SPLIT)),
    ]
    fo, fx, r_a, l_a, o_a, xf, xr, xl, xo, f_b, r_b, l_b, o_b = experts(
        pieces, own, other, shapes_out, 2 * n_z * n
    )

    bf = jnp.bfloat16
    back1, back2 = shift_z(fo, -1), shift_z(fx, 1)
    u_f = swap(xf, "xh")
    u_r, u_l, u_o = swap(xr, "xh"), swap(xl, "xh"), swap(xo, "xh")
    r_a = jnp.concatenate([plus(r_a[:n], back1), plus(r_a[n:])]).astype(bf)
    l_a = jnp.concatenate([plus(l_a[:n]), plus(l_a[n:], back2)]).astype(bf)
    s_a = plus(o_a, shift_z(r_a, -1), shift_z(l_a, 1))
    part_a = plus(s_a[:n], swap(s_a[n:].astype(bf), "xh"))
    f_b = plus(f_b, u_f).astype(bf)
    v1, v2 = shift_z(f_b[:, :half], -1), shift_z(f_b[:, half:], 1)
    r_b, l_b = plus(r_b, u_r), plus(l_b, u_l)
    r_b = jnp.concatenate([plus(r_b[:, :half], v1), r_b[:, half:]], axis=1).astype(bf)
    l_b = jnp.concatenate([l_b[:, :half], plus(l_b[:, half:], v2)], axis=1).astype(bf)
    part_b = plus(o_b, u_o, shift_z(r_b, -1), shift_z(l_b, 1))
    summed = jnp.concatenate([part_a, part_b], axis=1).astype(bf)
    returned = lax.all_to_all(summed, TENSOR, split_axis=0, concat_axis=0, tiled=True)
    mixture = jnp.dot(
        combine,
        returned.astype(jnp.float32),
        precision=lax.Precision.HIGHEST,
        preferred_element_type=jnp.float32,
    )
    layer_out = (resid + mixture).astype(jnp.bfloat16)

    ring_c = swap(ring, "c")
    wanted = my_group * seqs + lax.broadcasted_iota(jnp.int32, (seqs, 1), 0)
    seq_iota = lax.broadcasted_iota(jnp.int32, (seqs, new_slots.shape[0]), 1)
    source = jnp.sum(jnp.where(new_slots[None, :] == wanted, seq_iota, 0), axis=1)
    from_group = source // seqs
    dz = (lax.axis_index("z") - from_group // 4) % n_z
    dx = (from_group // 2 % 2) ^ lax.axis_index("xh")
    dc = (from_group % 2) ^ lax.axis_index("c")
    pick = jnp.stack([dc, dz * 2 + dx, source % seqs], axis=1).reshape(-1).astype(jnp.int32)
    new_codes, scales = store_blocks(pick, ring, ring_c, seqs)
    new_scales = jnp.swapaxes(scales[:, :, :1], 0, 1).astype(jnp.bfloat16)
    return (layer_out, new_codes, new_scales)


def solution(mesh):
    fine = Mesh(mesh.devices.reshape(4, 2, 2, 2, 4), GROUP + TENSOR)
    placed = (
        P(GROUP + TENSOR, None),
        P(GROUP, TENSOR),
        P(None, GROUP, TENSOR),
        P(None, GROUP, TENSOR),
        P(None, GROUP, TENSOR),
        P(),
        P(),
        P(TENSOR, None),
        P(),
        P(GROUP + TENSOR, None),
        P(GROUP + TENSOR),
        P(TENSOR, GROUP, None),
        P(TENSOR, GROUP, None),
        P(TENSOR, GROUP, None),
        P(),
    )
    return jax.shard_map(
        local,
        mesh=fine,
        in_specs=placed,
        out_specs=(
            P(GROUP + TENSOR, None),
            P(None, GROUP, TENSOR),
            P(None, GROUP, TENSOR),
        ),
        check_vma=False,
    )
```

```python
import functools
import math

import jax
import jax.numpy as jnp
from jax import lax
from jax.experimental import pallas as pl
from jax.experimental.pallas import tpu as pltpu
from jax.sharding import Mesh
from jax.sharding import PartitionSpec as P


EXPERTS = 8
TOP = 2
SUFFIX = 128
CAP = 12
GROUP = ("z", "xh", "c")
TENSOR = ("xl", "y")
SPLIT = 2048
PER = 4


def shift_z(x, by):
    n = lax.axis_size("z")
    return lax.ppermute(x, "z", [(i, (i + by) % n) for i in range(n)])


def swap(x, axis):
    return lax.ppermute(x, axis, [(0, 1), (1, 0)])


def plus(*terms):
    return sum(t.astype(jnp.float32) for t in terms)


def select_body(picked, scale_ref, codes_ref, *refs):
    outs, (pool_sc, sem) = refs[:-2], refs[-2:]
    pool = codes_ref.shape[1]
    for b in range(pool):
        for c in range(2):
            s = scale_ref[c, b, 0]
            pool_sc[b, c] = (codes_ref[c, b].astype(jnp.float32) * s).astype(jnp.bfloat16)
    copies, row = [], 0
    for i, out in enumerate(outs):
        rows = out.shape[2]
        for g in range(out.shape[0]):
            src = pool_sc.at[picked[g], :, pl.ds(row, rows)]
            copies.append(pltpu.make_async_copy(src, out.at[g], sem.at[i, g]))
        row += rows
    for copy in copies:
        copy.start()
    for copy in copies:
        copy.wait()


def select_blocks(picked, scales, codes, cuts):
    _, pool, rows, width = codes.shape
    groups = picked.shape[0]
    return pl.pallas_call(
        select_body,
        grid_spec=pltpu.PrefetchScalarGridSpec(
            num_scalar_prefetch=1,
            grid=(1,),
            in_specs=[
                pl.BlockSpec(memory_space=pltpu.SMEM),
                pl.BlockSpec(codes.shape, lambda i, p: (0, 0, 0, 0)),
            ],
            out_specs=[pl.BlockSpec(memory_space=pl.ANY)] * len(cuts),
            scratch_shapes=[
                pltpu.VMEM((pool, 2, rows, width), jnp.bfloat16),
                pltpu.SemaphoreType.DMA((len(cuts), groups)),
            ],
        ),
        out_shape=[jax.ShapeDtypeStruct((groups, 2, n, width), jnp.bfloat16) for n in cuts],
        cost_estimate=pl.CostEstimate(flops=1 << 20, bytes_accessed=6 << 20, transcendentals=0),
        name="select",
    )(picked, scales, codes)


def attend_body(begin, end, per, live, q_ref, new_ref, kv_ref, *refs):
    state, refs = (None, refs) if begin else (refs[:2], refs[2:])
    outs, refs = (refs[:1], refs[1:]) if end else (refs[:2], refs[2:])
    m_sc, acc_sc = refs[:2] if end else outs
    q_sc, v_sc = refs[-2:]
    step = pl.program_id(0)
    toks, dim = q_ref.shape[0], new_ref.shape[2]
    keys = kv_ref.shape[2]
    heads = q_ref.shape[1] // dim
    factor = math.log2(math.e) / math.sqrt(dim)
    nt = (((1,), (1,)), ((), ()))

    @pl.when(step == 0)
    def _():
        v_sc[:, dim:] = jnp.ones((v_sc.shape[0], dim), jnp.bfloat16)
        for h in range(heads):
            q_sc[h * toks : (h + 1) * toks] = q_ref[:, h * dim : (h + 1) * dim]
        if begin:
            v_sc[:toks, :dim] = new_ref[1]
            tok = lax.broadcasted_iota(jnp.int32, (toks, toks), 0)
            key = lax.broadcasted_iota(jnp.int32, (toks, toks), 1)
            seen = jnp.logical_and(tok // SUFFIX == key // SUFFIX, key <= tok)
            for h in range(heads):
                rows = slice(h * toks, (h + 1) * toks)
                s = lax.dot_general(q_sc[rows], new_ref[0], nt, preferred_element_type=jnp.float32)
                s = jnp.where(seen, s * factor, -1e30)
                m = jnp.max(s, axis=1, keepdims=True)
                p = jnp.exp2(s - m).astype(jnp.bfloat16)
                m_sc[rows] = jnp.broadcast_to(m, (toks, dim))
                acc_sc[rows] = jnp.dot(p, v_sc[:toks], preferred_element_type=jnp.float32)
        else:
            m_sc[...] = state[0][...]
            acc_sc[...] = state[1][...]

    alive = [live[step * per + i] for i in range(per)]

    @pl.when(sum(alive) > 0)
    def _():
        for i in range(per):
            v_sc[i * keys : (i + 1) * keys, :dim] = kv_ref[i, 1]
        k = kv_ref[:, 0].reshape(per * keys, dim)
        if per > 1:
            part = lax.broadcasted_iota(jnp.int32, (1, per * keys), 1) // keys
            hide = jnp.zeros((1, per * keys), jnp.float32)
            for i in range(per):
                gone = jnp.where(alive[i] > 0, 0.0, -1e30).astype(jnp.float32)
                hide = jnp.where(part == i, gone, hide)
        for h in range(heads):
            rows = slice(h * toks, (h + 1) * toks)
            s = lax.dot_general(q_sc[rows], k, nt, preferred_element_type=jnp.float32) * factor
            if per > 1:
                s = s + hide
            old = m_sc[rows][:, :1]
            m = jnp.maximum(old, jnp.max(s, axis=1, keepdims=True))
            p = jnp.exp2(s - m).astype(jnp.bfloat16)
            m_sc[rows] = jnp.broadcast_to(m, (toks, dim))
            acc_sc[rows] = acc_sc[rows] * jnp.exp2(old - m) + jnp.dot(
                p, v_sc[: per * keys], preferred_element_type=jnp.float32
            )

    if end:

        @pl.when(step == pl.num_programs(0) - 1)
        def _():
            for h in range(heads):
                rows = slice(h * toks, (h + 1) * toks)
                outs[0][:, h * dim : (h + 1) * dim] = (
                    acc_sc[rows][:, :dim] / acc_sc[rows][:, dim:]
                ).astype(jnp.bfloat16)


def attention(live, queries, new_kv, got, state, end, per):
    owners, _, rows, dim = got.shape
    toks, width = queries.shape
    whole = lambda shape: pl.BlockSpec(shape, lambda i, p: (0,) * len(shape))
    total = width // dim * toks
    begin = state is None
    carried = [
        jax.ShapeDtypeStruct((total, dim), jnp.float32),
        jax.ShapeDtypeStruct((total, 2 * dim), jnp.float32),
    ]
    results = [jax.ShapeDtypeStruct(queries.shape, jnp.bfloat16)] if end else carried
    return pl.pallas_call(
        functools.partial(attend_body, begin, end, per),
        grid_spec=pltpu.PrefetchScalarGridSpec(
            num_scalar_prefetch=1,
            grid=(owners // per,),
            in_specs=[
                whole(queries.shape),
                whole(new_kv.shape),
                pl.BlockSpec((per, 2, rows, dim), lambda i, p: (i, 0, 0, 0)),
            ]
            + ([] if begin else [whole(c.shape) for c in carried]),
            out_specs=[whole(r.shape) for r in results],
            scratch_shapes=([pltpu.VMEM(c.shape, c.dtype) for c in carried] if end else [])
            + [
                pltpu.VMEM((total, dim), jnp.bfloat16),
                pltpu.VMEM((max(per * rows, toks) if begin else per * rows, 2 * dim), jnp.bfloat16),
            ],
        ),
        out_shape=results,
        cost_estimate=pl.CostEstimate(
            flops=6 * total * rows * dim * owners,
            bytes_accessed=5 << 20,
            transcendentals=total * rows * owners,
        ),
        name="attend",
    )(live, queries, new_kv, got, *(() if begin else state))


def store_body(pick, *refs):
    ins, (codes_ref, scale_ref) = refs[:-2], refs[-2:]
    at = pick[3 * pl.program_id(0)]
    for c in range(2):
        x = ins[0][0, c]
        for i in range(1, len(ins)):
            x = jnp.where(at == i, ins[i][0, c], x)
        x = x.astype(jnp.float32)
        top = jnp.max(jnp.max(jnp.abs(x), axis=0, keepdims=True), axis=1, keepdims=True)
        scale = (top + 1e-06).astype(jnp.bfloat16).astype(jnp.float32)
        codes_ref[c] = (x / scale).astype(jnp.bfloat16)
        scale_ref[0, c : c + 1] = jnp.broadcast_to(scale, (1, scale_ref.shape[2]))


def store_blocks(pick, gathered, seqs):
    _, _, _, dim = gathered[0].shape
    source = pl.BlockSpec((1, 2, SUFFIX, dim), lambda k, p: (p[3 * k + 1], 0, p[3 * k + 2], 0))
    return pl.pallas_call(
        store_body,
        grid_spec=pltpu.PrefetchScalarGridSpec(
            num_scalar_prefetch=1,
            grid=(seqs,),
            in_specs=[source] * len(gathered),
            out_specs=[
                pl.BlockSpec((2, SUFFIX, dim), lambda k, p: (0, k, 0)),
                pl.BlockSpec((1, 2, dim), lambda k, p: (k, 0, 0)),
            ],
        ),
        out_shape=[
            jax.ShapeDtypeStruct((2, seqs * SUFFIX, dim), jnp.bfloat16),
            jax.ShapeDtypeStruct((seqs, 2, dim), jnp.float32),
        ],
        cost_estimate=pl.CostEstimate(flops=1 << 17, bytes_accessed=1 << 18, transcendentals=0),
        name="store",
    )(pick, *gathered)


def hidden_body(moves, *refs):
    n_in = len(moves)
    ins, refs = refs[:n_in], refs[n_in:]
    own, other, (out_ref, x_sc, sem) = refs[:2], refs[2:4], refs[4:]
    step, steps = pl.program_id(0), pl.num_programs(0)
    nt = (((1,), (1,)), ((), ()))

    @pl.when(step == 0)
    def _():
        copies = []
        for i, (ref, (r, c)) in enumerate(zip(ins, moves)):
            dst = x_sc.at[pl.ds(r, ref.shape[0]), pl.ds(c, ref.shape[1])]
            copies.append(pltpu.make_async_copy(ref, dst, sem.at[i]))
        for copy in copies:
            copy.start()
        for copy in copies:
            copy.wait()

    def run(gate, up):
        x = x_sc[...]
        g = lax.dot_general(x, gate[0], nt, preferred_element_type=jnp.float32)
        u = lax.dot_general(x, up[0], nt, preferred_element_type=jnp.float32)
        out_ref[...] = (g / (1.0 + jnp.exp(-g)) * u).astype(jnp.bfloat16)

    @pl.when(step < steps // 2)
    def _():
        run(*own)

    @pl.when(step >= steps // 2)
    def _():
        run(*other)


def hidden_units(pieces, own, other, rows, tile=256):
    _, units, width = own[0].shape
    half = units // tile
    first = pl.BlockSpec((1, tile, width), lambda i: (0, jnp.minimum(i, half - 1), 0))
    second = pl.BlockSpec((1, tile, width), lambda i: (0, jnp.maximum(i - half, 0), 0))
    ins, moves = zip(*pieces)
    return pl.pallas_call(
        functools.partial(hidden_body, moves),
        grid=(2 * half,),
        in_specs=[pl.BlockSpec(memory_space=pl.ANY)] * len(ins) + [first] * 2 + [second] * 2,
        out_specs=pl.BlockSpec((rows, tile), lambda i: (0, i)),
        out_shape=jax.ShapeDtypeStruct((rows, 2 * units), jnp.bfloat16),
        scratch_shapes=[
            pltpu.VMEM((rows, width), jnp.bfloat16),
            pltpu.SemaphoreType.DMA((len(ins),)),
        ],
        compiler_params=pltpu.CompilerParams(vmem_limit_bytes=56_000_000),
        cost_estimate=pl.CostEstimate(
            flops=8 * rows * units * width,
            bytes_accessed=8 * units * width + 2 * rows * width,
            transcendentals=2 * rows * units,
        ),
        name="hidden",
    )(*ins, *own[:2], *other[:2])


def down_body(moves, n_in, *refs):
    ins, (own, other), outs = refs[:n_in], refs[n_in : n_in + 2], refs[n_in + 2 :]
    units = own.shape[1]
    for of, ref in enumerate(ins):
        h = ref[...]
        y = jnp.dot(h[:, :units], own[0], preferred_element_type=jnp.float32)
        y += jnp.dot(h[:, units:], other[0], preferred_element_type=jnp.float32)
        y = y.astype(jnp.bfloat16)
        for out, places in zip(outs, moves):
            n = out.shape[0] // len(places)
            for i, (source, r) in enumerate(places):
                if source == of:
                    out[i * n : (i + 1) * n] = y[r : r + n]


def down_sums(hidden, own, other, start, size, shapes_out, tile=512):
    _, units, _ = own[2].shape
    weight = pl.BlockSpec((1, units, tile), lambda i: (0, 0, start // tile + i))
    rows, moves = zip(*shapes_out)
    total = sum(h.shape[0] for h in hidden)
    return pl.pallas_call(
        functools.partial(down_body, moves, len(hidden)),
        grid=(size // tile,),
        in_specs=[pl.BlockSpec(h.shape, lambda i: (0, 0)) for h in hidden] + [weight, weight],
        out_specs=[pl.BlockSpec((n, tile), lambda i: (0, i)) for n in rows],
        out_shape=[jax.ShapeDtypeStruct((n, size), jnp.bfloat16) for n in rows],
        compiler_params=pltpu.CompilerParams(vmem_limit_bytes=40_000_000),
        cost_estimate=pl.CostEstimate(
            flops=4 * total * units * size,
            bytes_accessed=4 * units * size + 2 * total * size + 4 * total * units,
            transcendentals=0,
        ),
        name="down",
    )(*hidden, own[2], other[2])


def local(
    hidden_in,
    queries,
    new_kv,
    pool_codes,
    pool_scales,
    block_table,
    prefix_blocks,
    out_proj,
    norm_gain,
    expert_ids,
    expert_share,
    gate_proj,
    up_proj,
    down_proj,
    new_slots,
):
    groups = lax.axis_size(GROUP)
    tensors = lax.axis_size(TENSOR)
    n_z = lax.axis_size("z")
    my_group = lax.axis_index(GROUP)
    pool = pool_scales.shape[1]
    dim = pool_codes.shape[2]
    pblock = pool_codes.shape[1] // pool
    group_tok = queries.shape[0]
    seqs = group_tok // SUFFIX
    model_width = hidden_in.shape[1]

    owners = block_table // pool
    position = lax.broadcasted_iota(jnp.int32, block_table.shape, 1)
    mine = jnp.logical_and(owners == my_group, position < prefix_blocks[:, None])
    picked = jnp.sum(jnp.where(mine, block_table % pool, 0), axis=1)
    (outgoing,) = select_blocks(
        picked, pool_scales, pool_codes.reshape(2, pool, pblock, dim), (pblock,)
    )
    got = lax.all_to_all(outgoing, GROUP, split_axis=0, concat_axis=0, tiled=True)
    my_row = lax.dynamic_index_in_dim(block_table, my_group, 0, keepdims=False)
    my_length = lax.dynamic_index_in_dim(prefix_blocks, my_group, 0, keepdims=False)
    row_live = lax.broadcasted_iota(jnp.int32, my_row.shape, 0) < my_length
    owner_iota = lax.broadcasted_iota(jnp.int32, (groups, my_row.shape[0]), 0)
    live = jnp.any(
        jnp.logical_and((my_row // pool)[None, :] == owner_iota, row_live[None, :]), axis=1
    ).astype(jnp.int32)

    fresh = jnp.stack([new_kv, swap(new_kv, "c")])
    fresh = jnp.concatenate([fresh, swap(fresh, "xh")])
    own = (gate_proj, up_proj, down_proj)
    own_late, got = lax.optimization_barrier((own, got))
    other = []
    for w in own_late:
        other.append(swap(w, "c"))

    (attn,) = attention(live, queries, new_kv, got, None, True, PER)
    partial = jnp.dot(attn, out_proj, preferred_element_type=jnp.float32).astype(jnp.bfloat16)
    partial = partial.reshape(tensors, group_tok // tensors, model_width)
    arrived = lax.all_to_all(partial, TENSOR, split_axis=0, concat_axis=0, tiled=True)
    gathered = [fresh]
    for k in range(1, n_z):
        gathered.append(shift_z(fresh, k))
    resid = hidden_in.astype(jnp.float32) + arrived.astype(jnp.float32).sum(axis=0)
    normed = (
        resid * lax.rsqrt(jnp.mean(resid * resid, axis=1, keepdims=True) + 1e-05) * norm_gain
    ).astype(jnp.bfloat16)

    tok_dev = group_tok // tensors
    pair_ids = expert_ids.reshape(-1)
    onehot = (
        pair_ids[:, None] == lax.broadcasted_iota(jnp.int32, (pair_ids.shape[0], EXPERTS), 1)
    ).astype(jnp.int32)
    rank = jnp.sum(onehot * (jnp.cumsum(onehot, axis=0) - 1), axis=1)
    slot = (pair_ids * CAP + rank).reshape(tok_dev, TOP)
    slot_iota = lax.broadcasted_iota(jnp.int32, (EXPERTS * CAP,), 0)
    matches = slot[:, :, None] == slot_iota[None, None, :]
    route_rows = jnp.any(matches, axis=1).astype(jnp.bfloat16)
    pair_weight = jnp.stack([expert_share, 1.0 - expert_share], axis=1)
    combine = jnp.sum(jnp.where(matches, pair_weight[:, :, None], 0.0), axis=1)
    outbound = jnp.einsum(
        "ie,id->ed", route_rows, normed, preferred_element_type=jnp.float32
    ).astype(jnp.bfloat16)
    landed = lax.all_to_all(outbound, TENSOR, split_axis=0, concat_axis=0, tiled=True)

    n = landed.shape[0]
    a, b = landed[:, :SPLIT], landed[:, SPLIT:]
    wide = model_width - SPLIT
    half = wide // 2
    ax = swap(a, "xh")
    b_r = shift_z(b, 1)
    b_l = shift_z(b, -1)
    bx = swap(b, "xh")
    a2 = jnp.concatenate([a, ax])
    a_r = shift_z(a2, 1)
    a_l = shift_z(a2, -1)
    bx_rl = swap(jnp.concatenate([b_r, b_l]), "xh")
    b_f1 = shift_z(b_r[:, :half], 1)
    b_f2 = shift_z(b_l[:, half:], -1)
    bx_f = swap(jnp.concatenate([b_f1, b_f2], axis=1), "xh")
    a_f1 = shift_z(a_r[:n], 1)
    a_f2 = shift_z(a_l[n:], -1)

    A, B = SPLIT, wide
    h_o = hidden_units([(a2, (0, 0)), (b, (0, A)), (bx, (n, A))], own, other, 2 * n)
    h_r = hidden_units(
        [(a_r, (0, 0)), (a_l, (2 * n, 0)), (a_f1, (4 * n, 0)), (a_f2, (5 * n, 0))]
        + [(b_r, (0, A)), (b_l, (2 * n, A))]
        + [(bx_rl[:n], (n, A)), (bx_rl[n:], (3 * n, A))]
        + [(b_f1, (4 * n, A)), (b_f2, (4 * n, A + half)), (bx_f, (5 * n, A))],
        own,
        other,
        6 * n,
    )
    o_b, r_b, l_b, f_b, x_o, x_rl, x_f = down_sums(
        [h_o, h_r],
        own,
        other,
        A,
        B,
        [(n, ((0, 0),)), (n, ((1, 0),)), (n, ((1, 2 * n),)), (n, ((1, 4 * n),))]
        + [(n, ((0, n),)), (2 * n, ((1, n), (1, 3 * n))), (n, ((1, 5 * n),))],
    )
    o_a, r_a, l_a, f1_a, f2_a = down_sums(
        [h_o, h_r],
        own,
        other,
        0,
        A,
        [(2 * n, ((0, 0),)), (2 * n, ((1, 0),)), (2 * n, ((1, 2 * n),))]
        + [(n, ((1, 4 * n),)), (n, ((1, 5 * n),))],
    )

    bf = jnp.bfloat16
    u_o = swap(x_o, "xh")
    u_rl = swap(x_rl, "xh")
    u_f = swap(x_f, "xh")
    back1 = shift_z(f1_a, -1)
    back2 = shift_z(f2_a, 1)
    r_a = jnp.concatenate([plus(r_a[:n], back1), plus(r_a[n:])]).astype(bf)
    l_a = jnp.concatenate([plus(l_a[:n]), plus(l_a[n:], back2)]).astype(bf)
    t_r = shift_z(r_a, -1)
    t_l = shift_z(l_a, 1)
    s_a = plus(o_a, t_r, t_l)
    t_x = swap(s_a[n:].astype(bf), "xh")
    part_a = plus(s_a[:n], t_x)
    f_b = plus(f_b, u_f).astype(bf)
    v1 = shift_z(f_b[:, :half], -1)
    v2 = shift_z(f_b[:, half:], 1)
    r_b, l_b = plus(r_b, u_rl[:n]), plus(l_b, u_rl[n:])
    r_b = jnp.concatenate([plus(r_b[:, :half], v1), r_b[:, half:]], axis=1).astype(bf)
    l_b = jnp.concatenate([l_b[:, :half], plus(l_b[:, half:], v2)], axis=1).astype(bf)
    v_r = shift_z(r_b, -1)
    v_l = shift_z(l_b, 1)
    part_b = plus(o_b, u_o, v_r, v_l)
    summed = jnp.concatenate([part_a, part_b], axis=1).astype(bf)
    returned = lax.all_to_all(summed, TENSOR, split_axis=0, concat_axis=0, tiled=True)
    mixture = jnp.dot(
        combine,
        returned.astype(jnp.float32),
        precision=lax.Precision.HIGHEST,
        preferred_element_type=jnp.float32,
    )
    layer_out = (resid + mixture).astype(jnp.bfloat16)

    wanted = my_group * seqs + lax.broadcasted_iota(jnp.int32, (seqs, 1), 0)
    seq_iota = lax.broadcasted_iota(jnp.int32, (seqs, new_slots.shape[0]), 1)
    source = jnp.sum(jnp.where(new_slots[None, :] == wanted, seq_iota, 0), axis=1)
    from_group = source // seqs
    dz = (lax.axis_index("z") - from_group // 4) % n_z
    dx = (from_group // 2 % 2) ^ lax.axis_index("xh")
    dc = (from_group % 2) ^ lax.axis_index("c")
    pick = jnp.stack([dz, dx * 2 + dc, source % seqs], axis=1).reshape(-1).astype(jnp.int32)
    new_codes, scales = store_blocks(pick, gathered, seqs)
    new_scales = jnp.swapaxes(scales[:, :, :1], 0, 1).astype(jnp.bfloat16)
    return (layer_out, new_codes, new_scales)


def solution(mesh):
    fine = Mesh(mesh.devices.reshape(4, 2, 2, 2, 4), GROUP + TENSOR)
    placed = (
        P(GROUP + TENSOR, None),
        P(GROUP, TENSOR),
        P(None, GROUP, TENSOR),
        P(None, GROUP, TENSOR),
        P(None, GROUP, TENSOR),
        P(),
        P(),
        P(TENSOR, None),
        P(),
        P(GROUP + TENSOR, None),
        P(GROUP + TENSOR),
        P(TENSOR, GROUP, None),
        P(TENSOR, GROUP, None),
        P(TENSOR, GROUP, None),
        P(),
    )
    return jax.shard_map(
        local,
        mesh=fine,
        in_specs=placed,
        out_specs=(
            P(GROUP + TENSOR, None),
            P(None, GROUP, TENSOR),
            P(None, GROUP, TENSOR),
        ),
        check_vma=False,
    )
```

```python
import functools
import math

import jax
import jax.numpy as jnp
from jax import lax
from jax.experimental import pallas as pl
from jax.experimental.pallas import tpu as pltpu
from jax.sharding import Mesh
from jax.sharding import PartitionSpec as P


EXPERTS = 8
TOP = 2
SUFFIX = 128
CAP = 12
GROUP = ("z", "xh", "c")
TENSOR = ("xl", "y")
PER = 4


def shift_z(x, by):
    n = lax.axis_size("z")
    return lax.ppermute(x, "z", [(i, (i + by) % n) for i in range(n)])


def swap(x, axis):
    return lax.ppermute(x, axis, [(0, 1), (1, 0)])


def plus(*terms):
    return sum(t.astype(jnp.float32) for t in terms)


def halved(routes):
    rows = routes.shape[0]
    routes = routes.reshape(rows, EXPERTS, CAP)
    none = jnp.zeros_like(routes)
    upper = jnp.concatenate([routes, none], axis=2).reshape(rows, -1)
    lower = jnp.concatenate([none, routes], axis=2).reshape(rows, -1)
    return jnp.concatenate([upper, lower])


def select_body(picked, scale_ref, codes_ref, *refs):
    outs, (pool_sc, sem) = refs[:-2], refs[-2:]
    pool = codes_ref.shape[1]
    for b in range(pool):
        for c in range(2):
            s = scale_ref[c, 0, b]
            pool_sc[b, c] = (codes_ref[c, b].astype(jnp.float32) * s).astype(jnp.bfloat16)
    copies, row = [], 0
    for i, out in enumerate(outs):
        rows = out.shape[2]
        for g in range(out.shape[0]):
            src = pool_sc.at[picked[g], :, pl.ds(row, rows)]
            copies.append(pltpu.make_async_copy(src, out.at[g], sem.at[i, g]))
        row += rows
    for copy in copies:
        copy.start()
    for copy in copies:
        copy.wait()


def select_blocks(picked, scales, codes, cuts):
    _, pool, rows, width = codes.shape
    groups = picked.shape[0]
    return pl.pallas_call(
        select_body,
        grid_spec=pltpu.PrefetchScalarGridSpec(
            num_scalar_prefetch=1,
            grid=(1,),
            in_specs=[
                pl.BlockSpec(memory_space=pltpu.SMEM),
                pl.BlockSpec(codes.shape, lambda i, p: (0, 0, 0, 0)),
            ],
            out_specs=[pl.BlockSpec(memory_space=pl.ANY)] * len(cuts),
            scratch_shapes=[
                pltpu.VMEM((pool, 2, rows, width), jnp.bfloat16),
                pltpu.SemaphoreType.DMA((len(cuts), groups)),
            ],
        ),
        out_shape=[jax.ShapeDtypeStruct((groups, 2, n, width), jnp.bfloat16) for n in cuts],
        cost_estimate=pl.CostEstimate(flops=1 << 20, bytes_accessed=6 << 20, transcendentals=0),
        name="select",
    )(picked, scales, codes)


def attend_body(begin, end, per, live, q_ref, new_ref, kv_ref, *refs):
    state, refs = (None, refs) if begin else (refs[:2], refs[2:])
    outs, refs = (refs[:1], refs[1:]) if end else (refs[:2], refs[2:])
    m_sc, acc_sc = refs[:2] if end else outs
    q_sc, v_sc = refs[-2:]
    step = pl.program_id(0)
    toks, dim = q_ref.shape[0], new_ref.shape[2]
    keys = kv_ref.shape[2]
    heads = q_ref.shape[1] // dim
    factor = math.log2(math.e) / math.sqrt(dim)
    nt = (((1,), (1,)), ((), ()))

    @pl.when(step == 0)
    def _():
        v_sc[:, dim:] = jnp.ones((v_sc.shape[0], dim), jnp.bfloat16)
        for h in range(heads):
            q_sc[h * toks : (h + 1) * toks] = q_ref[:, h * dim : (h + 1) * dim]
        if begin:
            v_sc[:toks, :dim] = new_ref[1]
            tok = lax.broadcasted_iota(jnp.int32, (toks, toks), 0)
            key = lax.broadcasted_iota(jnp.int32, (toks, toks), 1)
            seen = jnp.logical_and(tok // SUFFIX == key // SUFFIX, key <= tok)
            for h in range(heads):
                rows = slice(h * toks, (h + 1) * toks)
                s = lax.dot_general(q_sc[rows], new_ref[0], nt, preferred_element_type=jnp.float32)
                s = jnp.where(seen, s * factor, -1e30)
                m = jnp.max(s, axis=1, keepdims=True)
                p = jnp.exp2(s - m).astype(jnp.bfloat16)
                m_sc[rows] = jnp.broadcast_to(m, (toks, dim))
                acc_sc[rows] = jnp.dot(p, v_sc[:toks], preferred_element_type=jnp.float32)
        else:
            m_sc[...] = state[0][...]
            acc_sc[...] = state[1][...]

    alive = [live[step * per + i] for i in range(per)]

    @pl.when(sum(alive) > 0)
    def _():
        for i in range(per):
            v_sc[i * keys : (i + 1) * keys, :dim] = kv_ref[i, 1]
        k = kv_ref[:, 0].reshape(per * keys, dim)
        if per > 1:
            part = lax.broadcasted_iota(jnp.int32, (1, per * keys), 1) // keys
            hide = jnp.zeros((1, per * keys), jnp.float32)
            for i in range(per):
                gone = jnp.where(alive[i] > 0, 0.0, -1e30).astype(jnp.float32)
                hide = jnp.where(part == i, gone, hide)
        for h in range(heads):
            rows = slice(h * toks, (h + 1) * toks)
            s = lax.dot_general(q_sc[rows], k, nt, preferred_element_type=jnp.float32) * factor
            if per > 1:
                s = s + hide
            old = m_sc[rows][:, :1]
            m = jnp.maximum(old, jnp.max(s, axis=1, keepdims=True))
            p = jnp.exp2(s - m).astype(jnp.bfloat16)
            m_sc[rows] = jnp.broadcast_to(m, (toks, dim))
            acc_sc[rows] = acc_sc[rows] * jnp.exp2(old - m) + jnp.dot(
                p, v_sc[: per * keys], preferred_element_type=jnp.float32
            )

    if end:

        @pl.when(step == pl.num_programs(0) - 1)
        def _():
            for h in range(heads):
                rows = slice(h * toks, (h + 1) * toks)
                outs[0][:, h * dim : (h + 1) * dim] = (
                    acc_sc[rows][:, :dim] / acc_sc[rows][:, dim:]
                ).astype(jnp.bfloat16)


def attention(live, queries, new_kv, got, state, end, per):
    owners, _, rows, dim = got.shape
    toks, width = queries.shape
    whole = lambda shape: pl.BlockSpec(shape, lambda i, p: (0,) * len(shape))
    total = width // dim * toks
    begin = state is None
    carried = [
        jax.ShapeDtypeStruct((total, dim), jnp.float32),
        jax.ShapeDtypeStruct((total, 2 * dim), jnp.float32),
    ]
    results = [jax.ShapeDtypeStruct(queries.shape, jnp.bfloat16)] if end else carried
    return pl.pallas_call(
        functools.partial(attend_body, begin, end, per),
        grid_spec=pltpu.PrefetchScalarGridSpec(
            num_scalar_prefetch=1,
            grid=(owners // per,),
            in_specs=[
                whole(queries.shape),
                whole(new_kv.shape),
                pl.BlockSpec((per, 2, rows, dim), lambda i, p: (i, 0, 0, 0)),
            ]
            + ([] if begin else [whole(c.shape) for c in carried]),
            out_specs=[whole(r.shape) for r in results],
            scratch_shapes=([pltpu.VMEM(c.shape, c.dtype) for c in carried] if end else [])
            + [
                pltpu.VMEM((total, dim), jnp.bfloat16),
                pltpu.VMEM((max(per * rows, toks) if begin else per * rows, 2 * dim), jnp.bfloat16),
            ],
        ),
        out_shape=results,
        cost_estimate=pl.CostEstimate(
            flops=6 * total * rows * dim * owners,
            bytes_accessed=5 << 20,
            transcendentals=total * rows * owners,
        ),
        name="attend",
    )(live, queries, new_kv, got, *(() if begin else state))


def store_body(pick, *refs):
    ins, (codes_ref, scale_ref) = refs[:-2], refs[-2:]
    at = pick[3 * pl.program_id(0)]
    for c in range(2):
        x = ins[0][0, c]
        for i in range(1, len(ins)):
            x = jnp.where(at == i, ins[i][0, c], x)
        x = x.astype(jnp.float32)
        top = jnp.max(jnp.max(jnp.abs(x), axis=0, keepdims=True), axis=1, keepdims=True)
        scale = (top + 1e-06).astype(jnp.bfloat16).astype(jnp.float32)
        codes_ref[c] = (x / scale).astype(jnp.bfloat16)
        scale_ref[0, c : c + 1] = jnp.broadcast_to(scale, (1, scale_ref.shape[2]))


def store_blocks(pick, gathered, seqs):
    _, _, _, dim = gathered[0].shape
    source = pl.BlockSpec((1, 2, SUFFIX, dim), lambda k, p: (p[3 * k + 1], 0, p[3 * k + 2], 0))
    return pl.pallas_call(
        store_body,
        grid_spec=pltpu.PrefetchScalarGridSpec(
            num_scalar_prefetch=1,
            grid=(seqs,),
            in_specs=[source] * len(gathered),
            out_specs=[
                pl.BlockSpec((2, SUFFIX, dim), lambda k, p: (0, k, 0)),
                pl.BlockSpec((1, 2, dim), lambda k, p: (k, 0, 0)),
            ],
        ),
        out_shape=[
            jax.ShapeDtypeStruct((2, seqs * SUFFIX, dim), jnp.bfloat16),
            jax.ShapeDtypeStruct((seqs, 2, dim), jnp.float32),
        ],
        cost_estimate=pl.CostEstimate(flops=1 << 17, bytes_accessed=1 << 18, transcendentals=0),
        name="store",
    )(pick, *gathered)


def hidden_body(moves, *refs):
    n_in = len(moves)
    ins, refs = refs[:n_in], refs[n_in:]
    own, other, (out_ref, x_sc, sem) = refs[:2], refs[2:4], refs[4:]
    step, steps = pl.program_id(0), pl.num_programs(0)
    nt = (((1,), (1,)), ((), ()))

    @pl.when(step == 0)
    def _():
        copies = []
        for ref, (places, c) in zip(ins, moves):
            n = ref.shape[0] // len(places)
            for i, r in enumerate(places):
                src = ref.at[pl.ds(i * n, n)]
                dst = x_sc.at[pl.ds(r, n), pl.ds(c, ref.shape[1])]
                copies.append(pltpu.make_async_copy(src, dst, sem.at[len(copies)]))
        for copy in copies:
            copy.start()
        for copy in copies:
            copy.wait()

    def run(gate, up):
        x = x_sc[...]
        g = lax.dot_general(x, gate[0], nt, preferred_element_type=jnp.float32)
        u = lax.dot_general(x, up[0], nt, preferred_element_type=jnp.float32)
        out_ref[...] = (g / (1.0 + jnp.exp(-g)) * u).astype(jnp.bfloat16)

    @pl.when(step < steps // 2)
    def _():
        run(*own)

    @pl.when(step >= steps // 2)
    def _():
        run(*other)


def hidden_units(pieces, own, other, rows, tile=256):
    _, units, width = own[0].shape
    half = units // tile
    first = pl.BlockSpec((1, tile, width), lambda i: (0, jnp.minimum(i, half - 1), 0))
    second = pl.BlockSpec((1, tile, width), lambda i: (0, jnp.maximum(i - half, 0), 0))
    ins, moves = zip(*pieces)
    return pl.pallas_call(
        functools.partial(hidden_body, moves),
        grid=(2 * half,),
        in_specs=[pl.BlockSpec(memory_space=pl.ANY)] * len(ins) + [first] * 2 + [second] * 2,
        out_specs=pl.BlockSpec((rows, tile), lambda i: (0, i)),
        out_shape=jax.ShapeDtypeStruct((rows, 2 * units), jnp.bfloat16),
        scratch_shapes=[
            pltpu.VMEM((rows, width), jnp.bfloat16),
            pltpu.SemaphoreType.DMA((sum(len(m[0]) for m in moves),)),
        ],
        compiler_params=pltpu.CompilerParams(vmem_limit_bytes=56_000_000),
        cost_estimate=pl.CostEstimate(
            flops=8 * rows * units * width,
            bytes_accessed=8 * units * width + 2 * rows * width,
            transcendentals=2 * rows * units,
        ),
        name="hidden",
    )(*ins, *own[:2], *other[:2])


def down_body(moves, n_in, *refs):
    ins, (own, other), outs = refs[:n_in], refs[n_in : n_in + 2], refs[n_in + 2 :]
    units = own.shape[1]
    for of, ref in enumerate(ins):
        h = ref[...]
        y = jnp.dot(h[:, :units], own[0], preferred_element_type=jnp.float32)
        y += jnp.dot(h[:, units:], other[0], preferred_element_type=jnp.float32)
        y = y.astype(jnp.bfloat16)
        for out, places in zip(outs, moves):
            n = out.shape[0] // len(places)
            for i, (source, r) in enumerate(places):
                if source == of:
                    out[i * n : (i + 1) * n] = y[r : r + n]


def down_sums(hidden, own, other, start, size, shapes_out, tile=512):
    _, units, _ = own[2].shape
    weight = pl.BlockSpec((1, units, tile), lambda i: (0, 0, start // tile + i))
    rows, moves = zip(*shapes_out)
    total = sum(h.shape[0] for h in hidden)
    return pl.pallas_call(
        functools.partial(down_body, moves, len(hidden)),
        grid=(size // tile,),
        in_specs=[pl.BlockSpec(h.shape, lambda i: (0, 0)) for h in hidden] + [weight, weight],
        out_specs=[pl.BlockSpec((n, tile), lambda i: (0, i)) for n in rows],
        out_shape=[jax.ShapeDtypeStruct((n, size), jnp.bfloat16) for n in rows],
        compiler_params=pltpu.CompilerParams(vmem_limit_bytes=40_000_000),
        cost_estimate=pl.CostEstimate(
            flops=4 * total * units * size,
            bytes_accessed=4 * units * size + 2 * total * size + 4 * total * units,
            transcendentals=0,
        ),
        name="down",
    )(*hidden, own[2], other[2])


def local(
    hidden_in,
    queries,
    new_kv,
    pool_codes,
    pool_scales,
    block_table,
    prefix_blocks,
    out_proj,
    norm_gain,
    expert_ids,
    expert_share,
    gate_proj,
    up_proj,
    down_proj,
    new_slots,
):
    groups = lax.axis_size(GROUP)
    tensors = lax.axis_size(TENSOR)
    n_z = lax.axis_size("z")
    my_group = lax.axis_index(GROUP)
    pool = pool_scales.shape[1]
    dim = pool_codes.shape[2]
    pblock = pool_codes.shape[1] // pool
    group_tok = queries.shape[0]
    seqs = group_tok // SUFFIX
    model_width = hidden_in.shape[1]

    owners = block_table // pool
    position = lax.broadcasted_iota(jnp.int32, block_table.shape, 1)
    mine = jnp.logical_and(owners == my_group, position < prefix_blocks[:, None])
    picked = jnp.sum(jnp.where(mine, block_table % pool, 0), axis=1)
    (outgoing,) = select_blocks(
        picked, jnp.swapaxes(pool_scales, 1, 2), pool_codes.reshape(2, pool, pblock, dim), (pblock,)
    )
    got = lax.all_to_all(outgoing, GROUP, split_axis=0, concat_axis=0, tiled=True)
    my_row = lax.dynamic_index_in_dim(block_table, my_group, 0, keepdims=False)
    my_length = lax.dynamic_index_in_dim(prefix_blocks, my_group, 0, keepdims=False)
    row_live = lax.broadcasted_iota(jnp.int32, my_row.shape, 0) < my_length
    owner_iota = lax.broadcasted_iota(jnp.int32, (groups, my_row.shape[0]), 0)
    live = jnp.any(
        jnp.logical_and((my_row // pool)[None, :] == owner_iota, row_live[None, :]), axis=1
    ).astype(jnp.int32)

    fresh = jnp.stack([new_kv, swap(new_kv, "c")])
    fresh = jnp.concatenate([fresh, swap(fresh, "xh")])
    own = (gate_proj, up_proj, down_proj)
    own_late, got = lax.optimization_barrier((own, got))
    other = []
    for w in own_late:
        other.append(swap(w, "c"))

    (attn,) = attention(live, queries, new_kv, got, None, True, PER)
    partial = jnp.dot(attn, out_proj, preferred_element_type=jnp.float32).astype(jnp.bfloat16)
    partial = partial.reshape(tensors, group_tok // tensors, model_width)
    arrived = lax.all_to_all(partial, TENSOR, split_axis=0, concat_axis=0, tiled=True)
    gathered = [fresh]
    for k in range(1, n_z):
        gathered.append(shift_z(fresh, k))
    resid = hidden_in.astype(jnp.float32) + arrived.astype(jnp.float32).sum(axis=0)
    normed = (
        resid * lax.rsqrt(jnp.mean(resid * resid, axis=1, keepdims=True) + 1e-05) * norm_gain
    ).astype(jnp.bfloat16)

    tok_dev = group_tok // tensors
    pair_ids = expert_ids.reshape(-1)
    onehot = (
        pair_ids[:, None] == lax.broadcasted_iota(jnp.int32, (pair_ids.shape[0], EXPERTS), 1)
    ).astype(jnp.int32)
    rank = jnp.sum(onehot * (jnp.cumsum(onehot, axis=0) - 1), axis=1)
    slot = (pair_ids * CAP + rank).reshape(tok_dev, TOP)
    slot_iota = lax.broadcasted_iota(jnp.int32, (EXPERTS * CAP,), 0)
    matches = slot[:, :, None] == slot_iota[None, None, :]
    route_rows = halved(jnp.any(matches, axis=1).astype(jnp.bfloat16))
    pair_weight = jnp.stack([expert_share, 1.0 - expert_share], axis=1)
    combine = halved(jnp.sum(jnp.where(matches, pair_weight[:, :, None], 0.0), axis=1))
    half_width = model_width // 2
    both = jnp.concatenate([normed[:, :half_width], normed[:, half_width:]])
    outbound = jnp.einsum("ie,id->ed", route_rows, both, preferred_element_type=jnp.float32)
    landed = lax.all_to_all(
        outbound.astype(jnp.bfloat16).reshape(tensors, 2 * CAP, half_width),
        TENSOR,
        split_axis=0,
        concat_axis=0,
        tiled=True,
    )
    n = tensors * CAP
    a, b = landed[:, :CAP].reshape(n, half_width), landed[:, CAP:].reshape(n, half_width)
    half = half_width // 2
    ax = swap(a, "xh")
    b_r = shift_z(b, 1)
    b_l = shift_z(b, -1)
    bx = swap(b, "xh")
    a_r = shift_z(a, 1)
    a_l = shift_z(a, -1)
    ax_r = shift_z(ax, 1)
    ax_l = shift_z(ax, -1)
    bx_rl = swap(jnp.concatenate([b_r, b_l]), "xh")
    b_f1 = shift_z(b_r[:, :half], 1)
    b_f2 = shift_z(b_l[:, half:], -1)
    bx_f = swap(jnp.concatenate([b_f1, b_f2], axis=1), "xh")
    a_f1 = shift_z(a_r, 1)
    a_f2 = shift_z(ax_l, -1)

    w = half_width
    h_o = hidden_units(
        [(a, ((0,), 0)), (ax, ((n,), 0)), (b, ((0,), w)), (bx, ((n,), w))], own, other, 2 * n
    )
    h_r = hidden_units(
        [(a_r, ((0,), 0)), (ax_r, ((n,), 0)), (a_l, ((2 * n,), 0)), (ax_l, ((3 * n,), 0))]
        + [(a_f1, ((4 * n,), 0)), (a_f2, ((5 * n,), 0)), (b_r, ((0,), w)), (b_l, ((2 * n,), w))]
        + [(bx_rl, ((n, 3 * n), w)), (b_f1, ((4 * n,), w)), (b_f2, ((4 * n,), w + half))]
        + [(bx_f, ((5 * n,), w))],
        own,
        other,
        6 * n,
    )
    o_b, r_b, l_b, f_b, x_o, x_rl, x_f = down_sums(
        [h_o, h_r],
        own,
        other,
        w,
        w,
        [(n, ((0, 0),)), (n, ((1, 0),)), (n, ((1, 2 * n),)), (n, ((1, 4 * n),))]
        + [(n, ((0, n),)), (2 * n, ((1, n), (1, 3 * n))), (n, ((1, 5 * n),))],
    )
    o_a, r_a, rx_a, l_a, lx_a, f1_a, f2_a = down_sums(
        [h_o, h_r],
        own,
        other,
        0,
        w,
        [(2 * n, ((0, 0),)), (n, ((1, 0),)), (n, ((1, n),)), (n, ((1, 2 * n),))]
        + [(n, ((1, 3 * n),)), (n, ((1, 4 * n),)), (n, ((1, 5 * n),))],
    )

    bf = jnp.bfloat16
    u_o = swap(x_o, "xh")
    u_rl = swap(x_rl, "xh")
    u_f = swap(x_f, "xh")
    back1 = shift_z(f1_a, -1)
    back2 = shift_z(f2_a, 1)
    r_a = jnp.concatenate([plus(r_a, back1).astype(bf), rx_a])
    l_a = jnp.concatenate([l_a, plus(lx_a, back2).astype(bf)])
    t_r = shift_z(r_a, -1)
    t_l = shift_z(l_a, 1)
    s_a = plus(o_a, t_r, t_l)
    t_x = swap(s_a[n:].astype(bf), "xh")
    part_a = plus(s_a[:n], t_x)
    f_b = plus(f_b, u_f).astype(bf)
    v1 = shift_z(f_b[:, :half], -1)
    v2 = shift_z(f_b[:, half:], 1)
    r_b, l_b = plus(r_b, u_rl[:n]), plus(l_b, u_rl[n:])
    r_b = jnp.concatenate([plus(r_b[:, :half], v1), r_b[:, half:]], axis=1).astype(bf)
    l_b = jnp.concatenate([l_b[:, :half], plus(l_b[:, half:], v2)], axis=1).astype(bf)
    v_r = shift_z(r_b, -1)
    v_l = shift_z(l_b, 1)
    part_b = plus(o_b, u_o, v_r, v_l).astype(bf)
    summed = jnp.stack([p.reshape(tensors, CAP, w) for p in (part_a.astype(bf), part_b)], axis=1)
    returned = lax.all_to_all(
        summed.reshape(tensors, 2 * CAP, w), TENSOR, split_axis=0, concat_axis=0, tiled=True
    )
    mixture = jnp.dot(
        combine,
        returned.reshape(2 * n, w).astype(jnp.float32),
        precision=lax.Precision.HIGHEST,
        preferred_element_type=jnp.float32,
    )
    mixture = jnp.concatenate([mixture[:tok_dev], mixture[tok_dev:]], axis=1)
    layer_out = (resid + mixture).astype(jnp.bfloat16)

    wanted = my_group * seqs + lax.broadcasted_iota(jnp.int32, (seqs, 1), 0)
    seq_iota = lax.broadcasted_iota(jnp.int32, (seqs, new_slots.shape[0]), 1)
    source = jnp.sum(jnp.where(new_slots[None, :] == wanted, seq_iota, 0), axis=1)
    from_group = source // seqs
    dz = (lax.axis_index("z") - from_group // 4) % n_z
    dx = (from_group // 2 % 2) ^ lax.axis_index("xh")
    dc = (from_group % 2) ^ lax.axis_index("c")
    pick = jnp.stack([dz, dx * 2 + dc, source % seqs], axis=1).reshape(-1).astype(jnp.int32)
    new_codes, scales = store_blocks(pick, gathered, seqs)
    new_scales = jnp.swapaxes(scales[:, :, :1], 0, 1).astype(jnp.bfloat16)
    return (layer_out, new_codes, new_scales)


def solution(mesh):
    fine = Mesh(mesh.devices.reshape(4, 2, 2, 2, 4), GROUP + TENSOR)
    placed = (
        P(GROUP + TENSOR, None),
        P(GROUP, TENSOR),
        P(None, GROUP, TENSOR),
        P(None, GROUP, TENSOR),
        P(None, GROUP, TENSOR),
        P(),
        P(),
        P(TENSOR, None),
        P(),
        P(GROUP + TENSOR, None),
        P(GROUP + TENSOR),
        P(TENSOR, GROUP, None),
        P(TENSOR, GROUP, None),
        P(TENSOR, GROUP, None),
        P(),
    )
    return jax.shard_map(
        local,
        mesh=fine,
        in_specs=placed,
        out_specs=(
            P(GROUP + TENSOR, None),
            P(None, GROUP, TENSOR),
            P(None, GROUP, TENSOR),
        ),
        check_vma=False,
    )
```

```python
import functools
import math

import jax
import jax.numpy as jnp
from jax import lax
from jax.experimental import pallas as pl
from jax.experimental.pallas import tpu as pltpu
from jax.sharding import Mesh
from jax.sharding import PartitionSpec as P


EXPERTS = 8
TOP = 2
SUFFIX = 128
CAP = 12
GROUP = ("z", "xh", "c")
TENSOR = ("xl", "y")
PER = 4


def shift_z(x, by):
    n = lax.axis_size("z")
    return lax.ppermute(x, "z", [(i, (i + by) % n) for i in range(n)])


def swap(x, axis):
    return lax.ppermute(x, axis, [(0, 1), (1, 0)])


def plus(*terms):
    return sum(t.astype(jnp.float32) for t in terms)


def halved(routes):
    rows = routes.shape[0]
    routes = routes.reshape(rows, EXPERTS, CAP)
    none = jnp.zeros_like(routes)
    upper = jnp.concatenate([routes, none], axis=2).reshape(rows, -1)
    lower = jnp.concatenate([none, routes], axis=2).reshape(rows, -1)
    return jnp.concatenate([upper, lower])


def select_body(picked, scale_ref, codes_ref, *refs):
    outs, (pool_sc, sem) = refs[:-2], refs[-2:]
    pool = codes_ref.shape[1]
    for b in range(pool):
        for c in range(2):
            s = scale_ref[c, 0, b]
            pool_sc[b, c] = (codes_ref[c, b].astype(jnp.float32) * s).astype(jnp.bfloat16)
    copies, row = [], 0
    for i, out in enumerate(outs):
        rows = out.shape[2]
        for g in range(out.shape[0]):
            src = pool_sc.at[picked[g], :, pl.ds(row, rows)]
            copies.append(pltpu.make_async_copy(src, out.at[g], sem.at[i, g]))
        row += rows
    for copy in copies:
        copy.start()
    for copy in copies:
        copy.wait()


def select_blocks(picked, scales, codes, cuts):
    _, pool, rows, width = codes.shape
    groups = picked.shape[0]
    return pl.pallas_call(
        select_body,
        grid_spec=pltpu.PrefetchScalarGridSpec(
            num_scalar_prefetch=1,
            grid=(1,),
            in_specs=[
                pl.BlockSpec(memory_space=pltpu.SMEM),
                pl.BlockSpec(codes.shape, lambda i, p: (0, 0, 0, 0)),
            ],
            out_specs=[pl.BlockSpec(memory_space=pl.ANY)] * len(cuts),
            scratch_shapes=[
                pltpu.VMEM((pool, 2, rows, width), jnp.bfloat16),
                pltpu.SemaphoreType.DMA((len(cuts), groups)),
            ],
        ),
        out_shape=[jax.ShapeDtypeStruct((groups, 2, n, width), jnp.bfloat16) for n in cuts],
        cost_estimate=pl.CostEstimate(flops=1 << 20, bytes_accessed=6 << 20, transcendentals=0),
        name="select",
    )(picked, scales, codes)


def attend_body(begin, end, per, live, q_ref, new_ref, kv_ref, *refs):
    state, refs = (None, refs) if begin else (refs[:2], refs[2:])
    outs, refs = (refs[:1], refs[1:]) if end else (refs[:2], refs[2:])
    m_sc, acc_sc = refs[:2] if end else outs
    q_sc, v_sc = refs[-2:]
    step = pl.program_id(0)
    toks, dim = q_ref.shape[0], new_ref.shape[2]
    keys = kv_ref.shape[2]
    heads = q_ref.shape[1] // dim
    factor = math.log2(math.e) / math.sqrt(dim)
    nt = (((1,), (1,)), ((), ()))

    @pl.when(step == 0)
    def _():
        v_sc[:, dim:] = jnp.ones((v_sc.shape[0], dim), jnp.bfloat16)
        for h in range(heads):
            q_sc[h * toks : (h + 1) * toks] = q_ref[:, h * dim : (h + 1) * dim]
        if begin:
            v_sc[:toks, :dim] = new_ref[1]
            tok = lax.broadcasted_iota(jnp.int32, (toks, toks), 0)
            key = lax.broadcasted_iota(jnp.int32, (toks, toks), 1)
            seen = jnp.logical_and(tok // SUFFIX == key // SUFFIX, key <= tok)
            for h in range(heads):
                rows = slice(h * toks, (h + 1) * toks)
                s = lax.dot_general(q_sc[rows], new_ref[0], nt, preferred_element_type=jnp.float32)
                s = jnp.where(seen, s * factor, -1e30)
                m = jnp.max(s, axis=1, keepdims=True)
                p = jnp.exp2(s - m).astype(jnp.bfloat16)
                m_sc[rows] = jnp.broadcast_to(m, (toks, dim))
                acc_sc[rows] = jnp.dot(p, v_sc[:toks], preferred_element_type=jnp.float32)
        else:
            m_sc[...] = state[0][...]
            acc_sc[...] = state[1][...]

    alive = [live[step * per + i] for i in range(per)]

    @pl.when(sum(alive) > 0)
    def _():
        for i in range(per):
            v_sc[i * keys : (i + 1) * keys, :dim] = kv_ref[i, 1]
        k = kv_ref[:, 0].reshape(per * keys, dim)
        if per > 1:
            part = lax.broadcasted_iota(jnp.int32, (1, per * keys), 1) // keys
            hide = jnp.zeros((1, per * keys), jnp.float32)
            for i in range(per):
                gone = jnp.where(alive[i] > 0, 0.0, -1e30).astype(jnp.float32)
                hide = jnp.where(part == i, gone, hide)
        for h in range(heads):
            rows = slice(h * toks, (h + 1) * toks)
            s = lax.dot_general(q_sc[rows], k, nt, preferred_element_type=jnp.float32) * factor
            if per > 1:
                s = s + hide
            old = m_sc[rows][:, :1]
            m = jnp.maximum(old, jnp.max(s, axis=1, keepdims=True))
            p = jnp.exp2(s - m).astype(jnp.bfloat16)
            m_sc[rows] = jnp.broadcast_to(m, (toks, dim))
            acc_sc[rows] = acc_sc[rows] * jnp.exp2(old - m) + jnp.dot(
                p, v_sc[: per * keys], preferred_element_type=jnp.float32
            )

    if end:

        @pl.when(step == pl.num_programs(0) - 1)
        def _():
            for h in range(heads):
                rows = slice(h * toks, (h + 1) * toks)
                outs[0][:, h * dim : (h + 1) * dim] = (
                    acc_sc[rows][:, :dim] / acc_sc[rows][:, dim:]
                ).astype(jnp.bfloat16)


def attention(live, queries, new_kv, got, state, end, per):
    owners, _, rows, dim = got.shape
    toks, width = queries.shape
    whole = lambda shape: pl.BlockSpec(shape, lambda i, p: (0,) * len(shape))
    total = width // dim * toks
    begin = state is None
    carried = [
        jax.ShapeDtypeStruct((total, dim), jnp.float32),
        jax.ShapeDtypeStruct((total, 2 * dim), jnp.float32),
    ]
    results = [jax.ShapeDtypeStruct(queries.shape, jnp.bfloat16)] if end else carried
    return pl.pallas_call(
        functools.partial(attend_body, begin, end, per),
        grid_spec=pltpu.PrefetchScalarGridSpec(
            num_scalar_prefetch=1,
            grid=(owners // per,),
            in_specs=[
                whole(queries.shape),
                whole(new_kv.shape),
                pl.BlockSpec((per, 2, rows, dim), lambda i, p: (i, 0, 0, 0)),
            ]
            + ([] if begin else [whole(c.shape) for c in carried]),
            out_specs=[whole(r.shape) for r in results],
            scratch_shapes=([pltpu.VMEM(c.shape, c.dtype) for c in carried] if end else [])
            + [
                pltpu.VMEM((total, dim), jnp.bfloat16),
                pltpu.VMEM((max(per * rows, toks) if begin else per * rows, 2 * dim), jnp.bfloat16),
            ],
        ),
        out_shape=results,
        cost_estimate=pl.CostEstimate(
            flops=6 * total * rows * dim * owners,
            bytes_accessed=5 << 20,
            transcendentals=total * rows * owners,
        ),
        name="attend",
    )(live, queries, new_kv, got, *(() if begin else state))


def store_body(pick, *refs):
    ins, (codes_ref, scale_ref) = refs[:-2], refs[-2:]
    at = pick[3 * pl.program_id(0)]
    for c in range(2):
        x = ins[0][0, c]
        for i in range(1, len(ins)):
            x = jnp.where(at == i, ins[i][0, c], x)
        x = x.astype(jnp.float32)
        top = jnp.max(jnp.max(jnp.abs(x), axis=0, keepdims=True), axis=1, keepdims=True)
        scale = (top + 1e-06).astype(jnp.bfloat16).astype(jnp.float32)
        codes_ref[c] = (x / scale).astype(jnp.bfloat16)
        scale_ref[0, c : c + 1] = jnp.broadcast_to(scale, (1, scale_ref.shape[2]))


def store_blocks(pick, gathered, seqs):
    _, _, _, dim = gathered[0].shape
    source = pl.BlockSpec((1, 2, SUFFIX, dim), lambda k, p: (p[3 * k + 1], 0, p[3 * k + 2], 0))
    return pl.pallas_call(
        store_body,
        grid_spec=pltpu.PrefetchScalarGridSpec(
            num_scalar_prefetch=1,
            grid=(seqs,),
            in_specs=[source] * len(gathered),
            out_specs=[
                pl.BlockSpec((2, SUFFIX, dim), lambda k, p: (0, k, 0)),
                pl.BlockSpec((1, 2, dim), lambda k, p: (k, 0, 0)),
            ],
        ),
        out_shape=[
            jax.ShapeDtypeStruct((2, seqs * SUFFIX, dim), jnp.bfloat16),
            jax.ShapeDtypeStruct((seqs, 2, dim), jnp.float32),
        ],
        cost_estimate=pl.CostEstimate(flops=1 << 17, bytes_accessed=1 << 18, transcendentals=0),
        name="store",
    )(pick, *gathered)


def hidden_body(moves, *refs):
    n_in = len(moves)
    ins, refs = refs[:n_in], refs[n_in:]
    own, other, (out_ref, x_sc, sem) = refs[:2], refs[2:4], refs[4:]
    step, steps = pl.program_id(0), pl.num_programs(0)
    nt = (((1,), (1,)), ((), ()))

    @pl.when(step == 0)
    def _():
        copies = []
        for ref, (places, c) in zip(ins, moves):
            n = ref.shape[0] // len(places)
            for i, r in enumerate(places):
                src = ref.at[pl.ds(i * n, n)]
                dst = x_sc.at[pl.ds(r, n), pl.ds(c, ref.shape[1])]
                copies.append(pltpu.make_async_copy(src, dst, sem.at[len(copies)]))
        for copy in copies:
            copy.start()
        for copy in copies:
            copy.wait()

    def run(gate, up):
        x = x_sc[...]
        g = lax.dot_general(x, gate[0], nt, preferred_element_type=jnp.float32)
        u = lax.dot_general(x, up[0], nt, preferred_element_type=jnp.float32)
        out_ref[...] = (g / (1.0 + jnp.exp(-g)) * u).astype(jnp.bfloat16)

    @pl.when(step < steps // 2)
    def _():
        run(*own)

    @pl.when(step >= steps // 2)
    def _():
        run(*other)


def hidden_units(pieces, own, other, rows, tile=256):
    _, units, width = own[0].shape
    half = units // tile
    first = pl.BlockSpec((1, tile, width), lambda i: (0, jnp.minimum(i, half - 1), 0))
    second = pl.BlockSpec((1, tile, width), lambda i: (0, jnp.maximum(i - half, 0), 0))
    ins, moves = zip(*pieces)
    return pl.pallas_call(
        functools.partial(hidden_body, moves),
        grid=(2 * half,),
        in_specs=[pl.BlockSpec(memory_space=pl.ANY)] * len(ins) + [first] * 2 + [second] * 2,
        out_specs=pl.BlockSpec((rows, tile), lambda i: (0, i)),
        out_shape=jax.ShapeDtypeStruct((rows, 2 * units), jnp.bfloat16),
        scratch_shapes=[
            pltpu.VMEM((rows, width), jnp.bfloat16),
            pltpu.SemaphoreType.DMA((sum(len(m[0]) for m in moves),)),
        ],
        compiler_params=pltpu.CompilerParams(vmem_limit_bytes=48_500_000),
        cost_estimate=pl.CostEstimate(
            flops=8 * rows * units * width,
            bytes_accessed=8 * units * width + 2 * rows * width,
            transcendentals=2 * rows * units,
        ),
        name="hidden",
    )(*ins, *own[:2], *other[:2])


def down_body(moves, n_in, *refs):
    ins, (own, other), outs = refs[:n_in], refs[n_in : n_in + 2], refs[n_in + 2 :]
    units = own.shape[1]
    step, steps = pl.program_id(0), pl.num_programs(0)
    sums = []
    for ref in ins:
        h = ref[...]
        y = jnp.dot(h[:, :units], own[0], preferred_element_type=jnp.float32)
        y += jnp.dot(h[:, units:], other[0], preferred_element_type=jnp.float32)
        sums.append(y.astype(jnp.bfloat16))
    for part, here in enumerate((step < steps // 2, step >= steps // 2)):

        @pl.when(here)
        def _(part=part):
            for out, (of, places) in zip(outs, moves):
                n = out.shape[0] // len(places)
                for i, (source, r) in enumerate(places):
                    if of == part:
                        out[i * n : (i + 1) * n] = sums[source][r : r + n]


def down_sums(hidden, own, other, shapes_out, tile=1024):
    _, units, width = own[2].shape
    half = width // 2 // tile
    weight = pl.BlockSpec((1, units, tile), lambda i: (0, 0, i))
    columns = (lambda i: (0, jnp.minimum(i, half - 1)), lambda i: (0, jnp.maximum(i - half, 0)))
    moves = tuple((part, places) for part, _, places in shapes_out)
    total = sum(rows for _, rows, _ in hidden)
    return pl.pallas_call(
        functools.partial(down_body, moves, len(hidden)),
        grid=(2 * half,),
        in_specs=[
            pl.BlockSpec((rows, 2 * units), functools.partial(lambda at, i: (at, 0), at))
            for _, rows, at in hidden
        ]
        + [weight, weight],
        out_specs=[pl.BlockSpec((n, tile), columns[part]) for part, n, _ in shapes_out],
        out_shape=[jax.ShapeDtypeStruct((n, width // 2), jnp.bfloat16) for _, n, _ in shapes_out],
        compiler_params=pltpu.CompilerParams(vmem_limit_bytes=30_000_000),
        cost_estimate=pl.CostEstimate(
            flops=4 * total * units * width,
            bytes_accessed=4 * units * width + 2 * total * width + 4 * total * units,
            transcendentals=0,
        ),
        name="down",
    )(*[h for h, _, _ in hidden], own[2], other[2])


def local(
    hidden_in,
    queries,
    new_kv,
    pool_codes,
    pool_scales,
    block_table,
    prefix_blocks,
    out_proj,
    norm_gain,
    expert_ids,
    expert_share,
    gate_proj,
    up_proj,
    down_proj,
    new_slots,
):
    groups = lax.axis_size(GROUP)
    tensors = lax.axis_size(TENSOR)
    n_z = lax.axis_size("z")
    my_group = lax.axis_index(GROUP)
    pool = pool_scales.shape[1]
    dim = pool_codes.shape[2]
    pblock = pool_codes.shape[1] // pool
    group_tok = queries.shape[0]
    seqs = group_tok // SUFFIX
    model_width = hidden_in.shape[1]

    owners = block_table // pool
    position = lax.broadcasted_iota(jnp.int32, block_table.shape, 1)
    mine = jnp.logical_and(owners == my_group, position < prefix_blocks[:, None])
    picked = jnp.sum(jnp.where(mine, block_table % pool, 0), axis=1)
    (outgoing,) = select_blocks(
        picked, jnp.swapaxes(pool_scales, 1, 2), pool_codes.reshape(2, pool, pblock, dim), (pblock,)
    )
    got = lax.all_to_all(outgoing, GROUP, split_axis=0, concat_axis=0, tiled=True)
    my_row = lax.dynamic_index_in_dim(block_table, my_group, 0, keepdims=False)
    my_length = lax.dynamic_index_in_dim(prefix_blocks, my_group, 0, keepdims=False)
    row_live = lax.broadcasted_iota(jnp.int32, my_row.shape, 0) < my_length
    owner_iota = lax.broadcasted_iota(jnp.int32, (groups, my_row.shape[0]), 0)
    live = jnp.any(
        jnp.logical_and((my_row // pool)[None, :] == owner_iota, row_live[None, :]), axis=1
    ).astype(jnp.int32)

    fresh = jnp.stack([new_kv, swap(new_kv, "c")])
    fresh = jnp.concatenate([fresh, swap(fresh, "xh")])
    own = (gate_proj, up_proj, down_proj)
    own_late, got = lax.optimization_barrier((own, got))
    other = []
    for w in own_late:
        other.append(swap(w, "c"))

    (attn,) = attention(live, queries, new_kv, got, None, True, PER)
    partial = jnp.dot(attn, out_proj, preferred_element_type=jnp.float32).astype(jnp.bfloat16)
    partial = partial.reshape(tensors, group_tok // tensors, model_width)
    arrived = lax.all_to_all(partial, TENSOR, split_axis=0, concat_axis=0, tiled=True)
    gathered = [fresh]
    for k in range(1, n_z):
        gathered.append(shift_z(fresh, k))
    resid = hidden_in.astype(jnp.float32) + arrived.astype(jnp.float32).sum(axis=0)
    normed = (
        resid * lax.rsqrt(jnp.mean(resid * resid, axis=1, keepdims=True) + 1e-05) * norm_gain
    ).astype(jnp.bfloat16)

    tok_dev = group_tok // tensors
    pair_ids = expert_ids.reshape(-1)
    onehot = (
        pair_ids[:, None] == lax.broadcasted_iota(jnp.int32, (pair_ids.shape[0], EXPERTS), 1)
    ).astype(jnp.int32)
    rank = jnp.sum(onehot * (jnp.cumsum(onehot, axis=0) - 1), axis=1)
    slot = (pair_ids * CAP + rank).reshape(tok_dev, TOP)
    slot_iota = lax.broadcasted_iota(jnp.int32, (EXPERTS * CAP,), 0)
    matches = slot[:, :, None] == slot_iota[None, None, :]
    route_rows = halved(jnp.any(matches, axis=1).astype(jnp.bfloat16))
    pair_weight = jnp.stack([expert_share, 1.0 - expert_share], axis=1)
    combine = halved(jnp.sum(jnp.where(matches, pair_weight[:, :, None], 0.0), axis=1))
    half_width = model_width // 2
    both = jnp.concatenate([normed[:, :half_width], normed[:, half_width:]])
    outbound = jnp.einsum("ie,id->ed", route_rows, both, preferred_element_type=jnp.float32)
    landed = lax.all_to_all(
        outbound.astype(jnp.bfloat16).reshape(tensors, 2 * CAP, half_width),
        TENSOR,
        split_axis=0,
        concat_axis=0,
        tiled=True,
    )
    n = tensors * CAP
    a, b = landed[:, :CAP].reshape(n, half_width), landed[:, CAP:].reshape(n, half_width)
    half = half_width // 2
    ax = swap(a, "xh")
    b_r = shift_z(b, 1)
    b_l = shift_z(b, -1)
    bx = swap(b, "xh")
    a_r = shift_z(a, 1)
    a_l = shift_z(a, -1)
    ax_r = shift_z(ax, 1)
    ax_l = shift_z(ax, -1)
    bx_rl = swap(jnp.concatenate([b_r, b_l]), "xh")
    b_f1 = shift_z(b_r[:, :half], 1)
    b_f2 = shift_z(b_l[:, half:], -1)
    bx_f = swap(jnp.concatenate([b_f1, b_f2], axis=1), "xh")
    a_f1 = shift_z(a_r, 1)
    a_f2 = shift_z(ax_l, -1)

    w = half_width
    h_o = hidden_units(
        [(a, ((0,), 0)), (ax, ((n,), 0)), (b, ((0,), w)), (bx, ((n,), w))], own, other, 2 * n
    )
    h_r = hidden_units(
        [(a_r, ((0,), 0)), (ax_r, ((n,), 0)), (a_l, ((2 * n,), 0)), (ax_l, ((3 * n,), 0))]
        + [(a_f1, ((4 * n,), 0)), (a_f2, ((5 * n,), 0)), (b_r, ((0,), w)), (b_l, ((2 * n,), w))]
        + [(bx_rl, ((n, 3 * n), w)), (b_f1, ((4 * n,), w)), (b_f2, ((4 * n,), w + half))]
        + [(bx_f, ((5 * n,), w))],
        own,
        other,
        6 * n,
    )
    f1_a, f2_a, f_b, x_f = down_sums(
        [(h_r, 2 * n, 2)],
        own,
        other,
        [(0, n, ((0, 0),)), (0, n, ((0, n),)), (1, n, ((0, 0),)), (1, n, ((0, n),))],
    )
    o_a, r_a, rx_a, l_a, lx_a, o_b, r_b, l_b, x_o, x_rl = down_sums(
        [(h_o, 2 * n, 0), (h_r, 4 * n, 0)],
        own,
        other,
        [(0, 2 * n, ((0, 0),))]
        + [(0, n, ((1, r),)) for r in (0, n, 2 * n, 3 * n)]
        + [(1, n, ((0, 0),)), (1, n, ((1, 0),)), (1, n, ((1, 2 * n),)), (1, n, ((0, n),))]
        + [(1, 2 * n, ((1, n), (1, 3 * n)))],
    )

    bf = jnp.bfloat16
    u_o = swap(x_o, "xh")
    u_rl = swap(x_rl, "xh")
    u_f = swap(x_f, "xh")
    back1 = shift_z(f1_a, -1)
    back2 = shift_z(f2_a, 1)
    r_a = jnp.concatenate([plus(r_a, back1).astype(bf), rx_a])
    l_a = jnp.concatenate([l_a, plus(lx_a, back2).astype(bf)])
    t_r = shift_z(r_a, -1)
    t_l = shift_z(l_a, 1)
    s_a = plus(o_a, t_r, t_l)
    t_x = swap(s_a[n:].astype(bf), "xh")
    part_a = plus(s_a[:n], t_x)
    f_b = plus(f_b, u_f).astype(bf)
    v1 = shift_z(f_b[:, :half], -1)
    v2 = shift_z(f_b[:, half:], 1)
    r_b, l_b = plus(r_b, u_rl[:n]), plus(l_b, u_rl[n:])
    r_b = jnp.concatenate([plus(r_b[:, :half], v1), r_b[:, half:]], axis=1).astype(bf)
    l_b = jnp.concatenate([l_b[:, :half], plus(l_b[:, half:], v2)], axis=1).astype(bf)
    v_r = shift_z(r_b, -1)
    v_l = shift_z(l_b, 1)
    part_b = plus(o_b, u_o, v_r, v_l).astype(bf)
    summed = jnp.stack([p.reshape(tensors, CAP, w) for p in (part_a.astype(bf), part_b)], axis=1)
    returned = lax.all_to_all(
        summed.reshape(tensors, 2 * CAP, w), TENSOR, split_axis=0, concat_axis=0, tiled=True
    )
    mixture = jnp.dot(
        combine,
        returned.reshape(2 * n, w).astype(jnp.float32),
        precision=lax.Precision.HIGHEST,
        preferred_element_type=jnp.float32,
    )
    mixture = jnp.concatenate([mixture[:tok_dev], mixture[tok_dev:]], axis=1)
    layer_out = (resid + mixture).astype(jnp.bfloat16)

    wanted = my_group * seqs + lax.broadcasted_iota(jnp.int32, (seqs, 1), 0)
    seq_iota = lax.broadcasted_iota(jnp.int32, (seqs, new_slots.shape[0]), 1)
    source = jnp.sum(jnp.where(new_slots[None, :] == wanted, seq_iota, 0), axis=1)
    from_group = source // seqs
    dz = (lax.axis_index("z") - from_group // 4) % n_z
    dx = (from_group // 2 % 2) ^ lax.axis_index("xh")
    dc = (from_group % 2) ^ lax.axis_index("c")
    pick = jnp.stack([dz, dx * 2 + dc, source % seqs], axis=1).reshape(-1).astype(jnp.int32)
    new_codes, scales = store_blocks(pick, gathered, seqs)
    new_scales = jnp.swapaxes(scales[:, :, :1], 0, 1).astype(jnp.bfloat16)
    return (layer_out, new_codes, new_scales)


def solution(mesh):
    fine = Mesh(mesh.devices.reshape(4, 2, 2, 2, 4), GROUP + TENSOR)
    placed = (
        P(GROUP + TENSOR, None),
        P(GROUP, TENSOR),
        P(None, GROUP, TENSOR),
        P(None, GROUP, TENSOR),
        P(None, GROUP, TENSOR),
        P(),
        P(),
        P(TENSOR, None),
        P(),
        P(GROUP + TENSOR, None),
        P(GROUP + TENSOR),
        P(TENSOR, GROUP, None),
        P(TENSOR, GROUP, None),
        P(TENSOR, GROUP, None),
        P(),
    )
    return jax.shard_map(
        local,
        mesh=fine,
        in_specs=placed,
        out_specs=(
            P(GROUP + TENSOR, None),
            P(None, GROUP, TENSOR),
            P(None, GROUP, TENSOR),
        ),
        check_vma=False,
    )
```

```python
import functools
import math

import jax
import jax.numpy as jnp
from jax import lax
from jax.experimental import pallas as pl
from jax.experimental.pallas import tpu as pltpu
from jax.sharding import Mesh
from jax.sharding import PartitionSpec as P


EXPERTS = 8
TOP = 2
SUFFIX = 128
CAP = 12
GROUP = ("z", "xh", "c")
TENSOR = ("xl", "y")
PER = 4


def shift_z(x, by):
    n = lax.axis_size("z")
    return lax.ppermute(x, "z", [(i, (i + by) % n) for i in range(n)])


def swap(x, axis):
    return lax.ppermute(x, axis, [(0, 1), (1, 0)])


def plus(*terms):
    return sum(t.astype(jnp.float32) for t in terms)


def halved(routes):
    rows = routes.shape[0]
    routes = routes.reshape(rows, EXPERTS, CAP)
    none = jnp.zeros_like(routes)
    upper = jnp.concatenate([routes, none], axis=2).reshape(rows, -1)
    lower = jnp.concatenate([none, routes], axis=2).reshape(rows, -1)
    return jnp.concatenate([upper, lower])


def select_body(picked, scale_ref, codes_ref, *refs):
    outs, (pool_sc, sem) = refs[:-2], refs[-2:]
    pool = codes_ref.shape[1]
    for b in range(pool):
        for c in range(2):
            s = scale_ref[c, 0, b]
            pool_sc[b, c] = (codes_ref[c, b].astype(jnp.float32) * s).astype(jnp.bfloat16)
    copies, row = [], 0
    for i, out in enumerate(outs):
        rows = out.shape[2]
        for g in range(out.shape[0]):
            src = pool_sc.at[picked[g], :, pl.ds(row, rows)]
            copies.append(pltpu.make_async_copy(src, out.at[g], sem.at[i, g]))
        row += rows
    for copy in copies:
        copy.start()
    for copy in copies:
        copy.wait()


def select_blocks(picked, scales, codes, cuts):
    _, pool, rows, width = codes.shape
    groups = picked.shape[0]
    return pl.pallas_call(
        select_body,
        grid_spec=pltpu.PrefetchScalarGridSpec(
            num_scalar_prefetch=1,
            grid=(1,),
            in_specs=[
                pl.BlockSpec(memory_space=pltpu.SMEM),
                pl.BlockSpec(codes.shape, lambda i, p: (0, 0, 0, 0)),
            ],
            out_specs=[pl.BlockSpec(memory_space=pl.ANY)] * len(cuts),
            scratch_shapes=[
                pltpu.VMEM((pool, 2, rows, width), jnp.bfloat16),
                pltpu.SemaphoreType.DMA((len(cuts), groups)),
            ],
        ),
        out_shape=[jax.ShapeDtypeStruct((groups, 2, n, width), jnp.bfloat16) for n in cuts],
        cost_estimate=pl.CostEstimate(flops=1 << 20, bytes_accessed=6 << 20, transcendentals=0),
        name="select",
    )(picked, scales, codes)


def attend_body(begin, end, per, live, q_ref, new_ref, kv_ref, *refs):
    state, refs = (None, refs) if begin else (refs[:2], refs[2:])
    outs, refs = (refs[:1], refs[1:]) if end else (refs[:2], refs[2:])
    m_sc, acc_sc = refs[:2] if end else outs
    q_sc, v_sc = refs[-2:]
    step = pl.program_id(0)
    toks, dim = q_ref.shape[0], new_ref.shape[2]
    keys = kv_ref.shape[2]
    heads = q_ref.shape[1] // dim
    factor = math.log2(math.e) / math.sqrt(dim)
    nt = (((1,), (1,)), ((), ()))

    @pl.when(step == 0)
    def _():
        v_sc[:, dim:] = jnp.ones((v_sc.shape[0], dim), jnp.bfloat16)
        for h in range(heads):
            q_sc[h * toks : (h + 1) * toks] = q_ref[:, h * dim : (h + 1) * dim]
        if begin:
            v_sc[:toks, :dim] = new_ref[1]
            tok = lax.broadcasted_iota(jnp.int32, (toks, toks), 0)
            key = lax.broadcasted_iota(jnp.int32, (toks, toks), 1)
            seen = jnp.logical_and(tok // SUFFIX == key // SUFFIX, key <= tok)
            for h in range(heads):
                rows = slice(h * toks, (h + 1) * toks)
                s = lax.dot_general(q_sc[rows], new_ref[0], nt, preferred_element_type=jnp.float32)
                s = jnp.where(seen, s * factor, -1e30)
                m = jnp.max(s, axis=1, keepdims=True)
                p = jnp.exp2(s - m).astype(jnp.bfloat16)
                m_sc[rows] = jnp.broadcast_to(m, (toks, dim))
                acc_sc[rows] = jnp.dot(p, v_sc[:toks], preferred_element_type=jnp.float32)
        else:
            m_sc[...] = state[0][...]
            acc_sc[...] = state[1][...]

    alive = [live[step * per + i] for i in range(per)]

    @pl.when(sum(alive) > 0)
    def _():
        for i in range(per):
            v_sc[i * keys : (i + 1) * keys, :dim] = kv_ref[i, 1]
        k = kv_ref[:, 0].reshape(per * keys, dim)
        if per > 1:
            part = lax.broadcasted_iota(jnp.int32, (1, per * keys), 1) // keys
            hide = jnp.zeros((1, per * keys), jnp.float32)
            for i in range(per):
                gone = jnp.where(alive[i] > 0, 0.0, -1e30).astype(jnp.float32)
                hide = jnp.where(part == i, gone, hide)
        for h in range(heads):
            rows = slice(h * toks, (h + 1) * toks)
            s = lax.dot_general(q_sc[rows], k, nt, preferred_element_type=jnp.float32) * factor
            if per > 1:
                s = s + hide
            old = m_sc[rows][:, :1]
            m = jnp.maximum(old, jnp.max(s, axis=1, keepdims=True))
            p = jnp.exp2(s - m).astype(jnp.bfloat16)
            m_sc[rows] = jnp.broadcast_to(m, (toks, dim))
            acc_sc[rows] = acc_sc[rows] * jnp.exp2(old - m) + jnp.dot(
                p, v_sc[: per * keys], preferred_element_type=jnp.float32
            )

    if end:

        @pl.when(step == pl.num_programs(0) - 1)
        def _():
            for h in range(heads):
                rows = slice(h * toks, (h + 1) * toks)
                outs[0][:, h * dim : (h + 1) * dim] = (
                    acc_sc[rows][:, :dim] / acc_sc[rows][:, dim:]
                ).astype(jnp.bfloat16)


def attention(live, queries, new_kv, got, state, end, per):
    owners, _, rows, dim = got.shape
    toks, width = queries.shape
    whole = lambda shape: pl.BlockSpec(shape, lambda i, p: (0,) * len(shape))
    total = width // dim * toks
    begin = state is None
    carried = [
        jax.ShapeDtypeStruct((total, dim), jnp.float32),
        jax.ShapeDtypeStruct((total, 2 * dim), jnp.float32),
    ]
    results = [jax.ShapeDtypeStruct(queries.shape, jnp.bfloat16)] if end else carried
    return pl.pallas_call(
        functools.partial(attend_body, begin, end, per),
        grid_spec=pltpu.PrefetchScalarGridSpec(
            num_scalar_prefetch=1,
            grid=(owners // per,),
            in_specs=[
                whole(queries.shape),
                whole(new_kv.shape),
                pl.BlockSpec((per, 2, rows, dim), lambda i, p: (i, 0, 0, 0)),
            ]
            + ([] if begin else [whole(c.shape) for c in carried]),
            out_specs=[whole(r.shape) for r in results],
            scratch_shapes=([pltpu.VMEM(c.shape, c.dtype) for c in carried] if end else [])
            + [
                pltpu.VMEM((total, dim), jnp.bfloat16),
                pltpu.VMEM((max(per * rows, toks) if begin else per * rows, 2 * dim), jnp.bfloat16),
            ],
        ),
        out_shape=results,
        cost_estimate=pl.CostEstimate(
            flops=6 * total * rows * dim * owners,
            bytes_accessed=5 << 20,
            transcendentals=total * rows * owners,
        ),
        name="attend",
    )(live, queries, new_kv, got, *(() if begin else state))


def store_body(pick, *refs):
    ins, (codes_ref, scale_ref) = refs[:-2], refs[-2:]
    at = pick[3 * pl.program_id(0)]
    for c in range(2):
        x = ins[0][0, c]
        for i in range(1, len(ins)):
            x = jnp.where(at == i, ins[i][0, c], x)
        x = x.astype(jnp.float32)
        top = jnp.max(jnp.max(jnp.abs(x), axis=0, keepdims=True), axis=1, keepdims=True)
        scale = (top + 1e-06).astype(jnp.bfloat16).astype(jnp.float32)
        codes_ref[c] = (x / scale).astype(jnp.bfloat16)
        scale_ref[0, c : c + 1] = jnp.broadcast_to(scale, (1, scale_ref.shape[2]))


def store_blocks(pick, gathered, seqs):
    _, _, _, dim = gathered[0].shape
    source = pl.BlockSpec((1, 2, SUFFIX, dim), lambda k, p: (p[3 * k + 1], 0, p[3 * k + 2], 0))
    return pl.pallas_call(
        store_body,
        grid_spec=pltpu.PrefetchScalarGridSpec(
            num_scalar_prefetch=1,
            grid=(seqs,),
            in_specs=[source] * len(gathered),
            out_specs=[
                pl.BlockSpec((2, SUFFIX, dim), lambda k, p: (0, k, 0)),
                pl.BlockSpec((1, 2, dim), lambda k, p: (k, 0, 0)),
            ],
        ),
        out_shape=[
            jax.ShapeDtypeStruct((2, seqs * SUFFIX, dim), jnp.bfloat16),
            jax.ShapeDtypeStruct((seqs, 2, dim), jnp.float32),
        ],
        cost_estimate=pl.CostEstimate(flops=1 << 17, bytes_accessed=1 << 18, transcendentals=0),
        name="store",
    )(pick, *gathered)


def hidden_body(moves, *refs):
    n_in = len(moves)
    ins, refs = refs[:n_in], refs[n_in:]
    own, other, (out_ref, x_sc, sem) = refs[:2], refs[2:4], refs[4:]
    step, steps = pl.program_id(0), pl.num_programs(0)
    nt = (((1,), (1,)), ((), ()))

    @pl.when(step == 0)
    def _():
        copies = []
        for ref, (places, c) in zip(ins, moves):
            n = ref.shape[0] // len(places)
            for i, r in enumerate(places):
                src = ref.at[pl.ds(i * n, n)]
                dst = x_sc.at[pl.ds(r, n), pl.ds(c, ref.shape[1])]
                copies.append(pltpu.make_async_copy(src, dst, sem.at[len(copies)]))
        for copy in copies:
            copy.start()
        for copy in copies:
            copy.wait()

    def run(gate, up):
        x = x_sc[...]
        g = lax.dot_general(x, gate[0], nt, preferred_element_type=jnp.float32)
        u = lax.dot_general(x, up[0], nt, preferred_element_type=jnp.float32)
        out_ref[...] = (g / (1.0 + jnp.exp(-g)) * u).astype(jnp.bfloat16)

    @pl.when(step < steps // 2)
    def _():
        run(*own)

    @pl.when(step >= steps // 2)
    def _():
        run(*other)


def hidden_units(pieces, own, other, rows, limit, tile=256):
    _, units, width = own[0].shape
    half = units // tile
    first = pl.BlockSpec((1, tile, width), lambda i: (0, jnp.minimum(i, half - 1), 0))
    second = pl.BlockSpec((1, tile, width), lambda i: (0, jnp.maximum(i - half, 0), 0))
    ins, moves = zip(*pieces)
    return pl.pallas_call(
        functools.partial(hidden_body, moves),
        grid=(2 * half,),
        in_specs=[pl.BlockSpec(memory_space=pl.ANY)] * len(ins) + [first] * 2 + [second] * 2,
        out_specs=pl.BlockSpec((rows, tile), lambda i: (0, i)),
        out_shape=jax.ShapeDtypeStruct((rows, 2 * units), jnp.bfloat16),
        scratch_shapes=[
            pltpu.VMEM((rows, width), jnp.bfloat16),
            pltpu.SemaphoreType.DMA((sum(len(m[0]) for m in moves),)),
        ],
        compiler_params=pltpu.CompilerParams(vmem_limit_bytes=limit),
        cost_estimate=pl.CostEstimate(
            flops=8 * rows * units * width,
            bytes_accessed=8 * units * width + 2 * rows * width,
            transcendentals=2 * rows * units,
        ),
        name="hidden",
    )(*ins, *own[:2], *other[:2])


def down_body(moves, n_in, *refs):
    ins, (own, other), outs = refs[:n_in], refs[n_in : n_in + 2], refs[n_in + 2 :]
    units = own.shape[1]
    step, steps = pl.program_id(0), pl.num_programs(0)
    sums = []
    for ref in ins:
        h = ref[...]
        y = jnp.dot(h[:, :units], own[0], preferred_element_type=jnp.float32)
        y += jnp.dot(h[:, units:], other[0], preferred_element_type=jnp.float32)
        sums.append(y.astype(jnp.bfloat16))
    for part, here in enumerate((step < steps // 2, step >= steps // 2)):

        @pl.when(here)
        def _(part=part):
            for out, (of, places) in zip(outs, moves):
                n = out.shape[0] // len(places)
                for i, (source, r) in enumerate(places):
                    if of == part:
                        out[i * n : (i + 1) * n] = sums[source][r : r + n]


def down_sums(hidden, own, other, shapes_out, tile=1024):
    _, units, width = own[2].shape
    half = width // 2 // tile
    weight = pl.BlockSpec((1, units, tile), lambda i: (0, 0, i))
    columns = (lambda i: (0, jnp.minimum(i, half - 1)), lambda i: (0, jnp.maximum(i - half, 0)))
    moves = tuple((part, places) for part, _, places in shapes_out)
    total = sum(rows for _, rows, _ in hidden)
    return pl.pallas_call(
        functools.partial(down_body, moves, len(hidden)),
        grid=(2 * half,),
        in_specs=[
            pl.BlockSpec((rows, 2 * units), functools.partial(lambda at, i: (at, 0), at))
            for _, rows, at in hidden
        ]
        + [weight, weight],
        out_specs=[pl.BlockSpec((n, tile), columns[part]) for part, n, _ in shapes_out],
        out_shape=[jax.ShapeDtypeStruct((n, width // 2), jnp.bfloat16) for _, n, _ in shapes_out],
        compiler_params=pltpu.CompilerParams(vmem_limit_bytes=30_000_000),
        cost_estimate=pl.CostEstimate(
            flops=4 * total * units * width,
            bytes_accessed=4 * units * width + 2 * total * width + 4 * total * units,
            transcendentals=0,
        ),
        name="down",
    )(*[h for h, _, _ in hidden], own[2], other[2])


def local(
    hidden_in,
    queries,
    new_kv,
    pool_codes,
    pool_scales,
    block_table,
    prefix_blocks,
    out_proj,
    norm_gain,
    expert_ids,
    expert_share,
    gate_proj,
    up_proj,
    down_proj,
    new_slots,
):
    groups = lax.axis_size(GROUP)
    tensors = lax.axis_size(TENSOR)
    n_z = lax.axis_size("z")
    my_group = lax.axis_index(GROUP)
    pool = pool_scales.shape[1]
    dim = pool_codes.shape[2]
    pblock = pool_codes.shape[1] // pool
    group_tok = queries.shape[0]
    seqs = group_tok // SUFFIX
    model_width = hidden_in.shape[1]

    owners = block_table // pool
    position = lax.broadcasted_iota(jnp.int32, block_table.shape, 1)
    mine = jnp.logical_and(owners == my_group, position < prefix_blocks[:, None])
    picked = jnp.sum(jnp.where(mine, block_table % pool, 0), axis=1)
    (outgoing,) = select_blocks(
        picked, jnp.swapaxes(pool_scales, 1, 2), pool_codes.reshape(2, pool, pblock, dim), (pblock,)
    )
    got = lax.all_to_all(outgoing, GROUP, split_axis=0, concat_axis=0, tiled=True)
    my_row = lax.dynamic_index_in_dim(block_table, my_group, 0, keepdims=False)
    my_length = lax.dynamic_index_in_dim(prefix_blocks, my_group, 0, keepdims=False)
    row_live = lax.broadcasted_iota(jnp.int32, my_row.shape, 0) < my_length
    owner_iota = lax.broadcasted_iota(jnp.int32, (groups, my_row.shape[0]), 0)
    live = jnp.any(
        jnp.logical_and((my_row // pool)[None, :] == owner_iota, row_live[None, :]), axis=1
    ).astype(jnp.int32)

    fresh = jnp.stack([new_kv, swap(new_kv, "c")])
    fresh = jnp.concatenate([fresh, swap(fresh, "xh")])
    own = (gate_proj, up_proj, down_proj)
    own_late, got = lax.optimization_barrier((own, got))
    other = []
    for w in own_late:
        other.append(swap(w, "c"))

    (attn,) = attention(live, queries, new_kv, got, None, True, PER)
    partial = jnp.dot(attn, out_proj, preferred_element_type=jnp.float32).astype(jnp.bfloat16)
    partial = partial.reshape(tensors, group_tok // tensors, model_width)
    arrived = lax.all_to_all(partial, TENSOR, split_axis=0, concat_axis=0, tiled=True)
    gathered = [fresh]
    for k in range(1, n_z):
        gathered.append(shift_z(fresh, k))
    resid = hidden_in.astype(jnp.float32) + arrived.astype(jnp.float32).sum(axis=0)
    normed = (
        resid * lax.rsqrt(jnp.mean(resid * resid, axis=1, keepdims=True) + 1e-05) * norm_gain
    ).astype(jnp.bfloat16)

    tok_dev = group_tok // tensors
    pair_ids = expert_ids.reshape(-1)
    onehot = (
        pair_ids[:, None] == lax.broadcasted_iota(jnp.int32, (pair_ids.shape[0], EXPERTS), 1)
    ).astype(jnp.int32)
    rank = jnp.sum(onehot * (jnp.cumsum(onehot, axis=0) - 1), axis=1)
    slot = (pair_ids * CAP + rank).reshape(tok_dev, TOP)
    slot_iota = lax.broadcasted_iota(jnp.int32, (EXPERTS * CAP,), 0)
    matches = slot[:, :, None] == slot_iota[None, None, :]
    route_rows = halved(jnp.any(matches, axis=1).astype(jnp.bfloat16))
    pair_weight = jnp.stack([expert_share, 1.0 - expert_share], axis=1)
    combine = halved(jnp.sum(jnp.where(matches, pair_weight[:, :, None], 0.0), axis=1))
    half_width = model_width // 2
    both = jnp.concatenate([normed[:, :half_width], normed[:, half_width:]])
    outbound = jnp.einsum("ie,id->ed", route_rows, both, preferred_element_type=jnp.float32)
    landed = lax.all_to_all(
        outbound.astype(jnp.bfloat16).reshape(tensors, 2 * CAP, half_width),
        TENSOR,
        split_axis=0,
        concat_axis=0,
        tiled=True,
    )
    n = tensors * CAP
    a, b = landed[:, :CAP].reshape(n, half_width), landed[:, CAP:].reshape(n, half_width)
    half = half_width // 2
    ax = swap(a, "xh")
    b_r = shift_z(b, 1)
    b_l = shift_z(b, -1)
    bx = swap(b, "xh")
    a_r = shift_z(a, 1)
    a_l = shift_z(a, -1)
    ax_r = shift_z(ax, 1)
    ax_l = shift_z(ax, -1)
    bx_rl = swap(jnp.concatenate([b_r, b_l]), "xh")
    b_f1 = shift_z(b_r[:, :half], 1)
    b_f2 = shift_z(b_l[:, half:], -1)
    bx_f = swap(jnp.concatenate([b_f1, b_f2], axis=1), "xh")
    a_f1 = shift_z(a_r, 1)
    a_f2 = shift_z(ax_l, -1)

    w = half_width
    h_o = hidden_units(
        [(a, ((0,), 0)), (ax, ((n,), 0)), (b, ((0,), w)), (bx, ((n,), w))], own, other, 2 * n, 53_000_000
    )
    h_r = hidden_units(
        [(a_r, ((0,), 0)), (ax_r, ((n,), 0)), (a_l, ((2 * n,), 0)), (ax_l, ((3 * n,), 0))]
        + [(a_f1, ((4 * n,), 0)), (a_f2, ((5 * n,), 0)), (b_r, ((0,), w)), (b_l, ((2 * n,), w))]
        + [(bx_rl, ((n, 3 * n), w)), (b_f1, ((4 * n,), w)), (b_f2, ((4 * n,), w + half))]
        + [(bx_f, ((5 * n,), w))],
        own,
        other,
        6 * n,
        48_500_000,
    )
    f1_a, f2_a, f_b, x_f = down_sums(
        [(h_r, 2 * n, 2)],
        own,
        other,
        [(0, n, ((0, 0),)), (0, n, ((0, n),)), (1, n, ((0, 0),)), (1, n, ((0, n),))],
    )
    o_a, r_a, rx_a, l_a, lx_a, o_b, r_b, l_b, x_o, x_rl = down_sums(
        [(h_o, 2 * n, 0), (h_r, 4 * n, 0)],
        own,
        other,
        [(0, 2 * n, ((0, 0),))]
        + [(0, n, ((1, r),)) for r in (0, n, 2 * n, 3 * n)]
        + [(1, n, ((0, 0),)), (1, n, ((1, 0),)), (1, n, ((1, 2 * n),)), (1, n, ((0, n),))]
        + [(1, 2 * n, ((1, n), (1, 3 * n)))],
    )

    bf = jnp.bfloat16
    u_o = swap(x_o, "xh")
    u_rl = swap(x_rl, "xh")
    u_f = swap(x_f, "xh")
    back1 = shift_z(f1_a, -1)
    back2 = shift_z(f2_a, 1)
    r_a = jnp.concatenate([plus(r_a, back1).astype(bf), rx_a])
    l_a = jnp.concatenate([l_a, plus(lx_a, back2).astype(bf)])
    t_r = shift_z(r_a, -1)
    t_l = shift_z(l_a, 1)
    s_a = plus(o_a, t_r, t_l)
    t_x = swap(s_a[n:].astype(bf), "xh")
    part_a = plus(s_a[:n], t_x)
    f_b = plus(f_b, u_f).astype(bf)
    v1 = shift_z(f_b[:, :half], -1)
    v2 = shift_z(f_b[:, half:], 1)
    r_b, l_b = plus(r_b, u_rl[:n]), plus(l_b, u_rl[n:])
    r_b = jnp.concatenate([plus(r_b[:, :half], v1), r_b[:, half:]], axis=1).astype(bf)
    l_b = jnp.concatenate([l_b[:, :half], plus(l_b[:, half:], v2)], axis=1).astype(bf)
    v_r = shift_z(r_b, -1)
    v_l = shift_z(l_b, 1)
    part_b = plus(o_b, u_o, v_r, v_l).astype(bf)
    summed = jnp.stack([p.reshape(tensors, CAP, w) for p in (part_a.astype(bf), part_b)], axis=1)
    returned = lax.all_to_all(
        summed.reshape(tensors, 2 * CAP, w), TENSOR, split_axis=0, concat_axis=0, tiled=True
    )
    mixture = jnp.dot(
        combine,
        returned.reshape(2 * n, w).astype(jnp.float32),
        precision=lax.Precision.HIGHEST,
        preferred_element_type=jnp.float32,
    )
    mixture = jnp.concatenate([mixture[:tok_dev], mixture[tok_dev:]], axis=1)
    layer_out = (resid + mixture).astype(jnp.bfloat16)

    wanted = my_group * seqs + lax.broadcasted_iota(jnp.int32, (seqs, 1), 0)
    seq_iota = lax.broadcasted_iota(jnp.int32, (seqs, new_slots.shape[0]), 1)
    source = jnp.sum(jnp.where(new_slots[None, :] == wanted, seq_iota, 0), axis=1)
    from_group = source // seqs
    dz = (lax.axis_index("z") - from_group // 4) % n_z
    dx = (from_group // 2 % 2) ^ lax.axis_index("xh")
    dc = (from_group % 2) ^ lax.axis_index("c")
    pick = jnp.stack([dz, dx * 2 + dc, source % seqs], axis=1).reshape(-1).astype(jnp.int32)
    new_codes, scales = store_blocks(pick, gathered, seqs)
    new_scales = jnp.swapaxes(scales[:, :, :1], 0, 1).astype(jnp.bfloat16)
    return (layer_out, new_codes, new_scales)


def solution(mesh):
    fine = Mesh(mesh.devices.reshape(4, 2, 2, 2, 4), GROUP + TENSOR)
    placed = (
        P(GROUP + TENSOR, None),
        P(GROUP, TENSOR),
        P(None, GROUP, TENSOR),
        P(None, GROUP, TENSOR),
        P(None, GROUP, TENSOR),
        P(),
        P(),
        P(TENSOR, None),
        P(),
        P(GROUP + TENSOR, None),
        P(GROUP + TENSOR),
        P(TENSOR, GROUP, None),
        P(TENSOR, GROUP, None),
        P(TENSOR, GROUP, None),
        P(),
    )
    return jax.shard_map(
        local,
        mesh=fine,
        in_specs=placed,
        out_specs=(
            P(GROUP + TENSOR, None),
            P(None, GROUP, TENSOR),
            P(None, GROUP, TENSOR),
        ),
        check_vma=False,
    )
```
